256 devices in a mesh: dp: 32 (over x, z), comp: 8 (over y, core).
Axes of the slice: x: 4, y: 4, z: 8, core: 2. Of those that a mesh axis runs over, the one named last changes fastest.
Arguments:
- embeddings: float32 [32768, 1024], P('dp'), may hold values from -6 to 6
- means: float32 [8192, 1024], P(('comp', 'dp')), may hold values from -2 to 2
- variances: float32 [8192, 1024], P(('comp', 'dp')), may hold values from 0.7 to 1.4
- log_weights: float32 [8192], P(('comp', 'dp')), may hold values from -2 to 0
Outputs:
- new_means: float32 [8192, 1024], P(('comp', 'dp'))
- new_variances: float32 [8192, 1024], P(('comp', 'dp'))
- new_weights: float32 [8192], P(('comp', 'dp'))
- row_loglik: float32 [32768], P('dp')
The draws below stay inside these ranges and needn't reach their ends.
All inputs are finite; a program needn't handle non-finite values.
Results may differ from the reference program's by a relative error of at most 0.00045.
Values sent between devices are 32-bit elements; how exact they have to be, the bound alone decides.
A program may use at most 128 MiB of HBM per device.

```python
import math
import jax
import jax.numpy as jnp
from jax import lax

D = 1024
K = 8192
NROWS = 32768


def block_scale(stream_key, shape, cuts, least, high):
    def one(axis_at, blocks):
        steps = jax.random.uniform(jax.random.fold_in(jax.random.fold_in(stream_key, 6), axis_at), (blocks,), jnp.float32, least / len(cuts), high / len(cuts))
        return jnp.repeat(jnp.exp(steps), shape[axis_at] // blocks).reshape((-1,) + (1,) * (len(shape) - axis_at - 1))

    loudness = one(*cuts[0])
    for cut in cuts[1:]:
        loudness = loudness * one(*cut)
    return loudness


def normal_values(own_key, dims, scale, bound, cuts=(), dtype=jnp.bfloat16):
    gain = block_scale(own_key, dims, cuts, -0.22, 0.18) if cuts else 1.0
    entries = jax.random.normal(own_key, dims, jnp.float32) * scale * gain
    return jnp.minimum(jnp.maximum(entries, -bound), bound).astype(dtype)


def setup_inputs(seed: int = 0) -> dict:
    keys = jax.random.split(jax.random.key(seed), 5)
    return {
        "embeddings": normal_values(keys[0], (NROWS, D), 1.0, 6.0, ((0, 32),), jnp.float32),
        "means": normal_values(keys[1], (K, D), 0.15, 2.0, ((0, 256),), jnp.float32),
        "variances": jnp.clip(jnp.exp(math.log(1.4) - 0.6931472 * jax.random.uniform(keys[2], (K, D), jnp.float32) ** block_scale(keys[2], (K, D), ((0, 256),), -0.2, 0.2)), 0.7, 1.4),
        "log_weights": jnp.clip(-2.0 + 2.0 * jax.random.uniform(keys[3], (K,), jnp.float32) ** block_scale(keys[3], (K,), ((0, 256),), -0.2, 0.2), -2.0, 0.0),
    }


circle_log = 1.8378770664093453


def component_terms(means, variances, log_weights):
    precision = 1.0 / variances
    scaled = means * precision
    width = means.shape[1]
    offset = log_weights - 0.5 * jnp.sum(jnp.log(variances), axis=1) - 0.5 * jnp.sum(means * scaled, axis=1) - 0.5 * width * circle_log
    return precision, scaled, offset


def row_scores(block, squares, precision, scaled, offset):
    highest = lax.Precision.HIGHEST
    quad = jnp.dot(squares, precision.T, precision=highest, preferred_element_type=jnp.float32)
    cross = jnp.dot(block, scaled.T, precision=highest, preferred_element_type=jnp.float32)
    return offset[None, :] + cross - 0.5 * quad


def weighted_sum(resp, values):
    return lax.dot_general(resp, values, (((0,), (0,)), ((), ())), precision=lax.Precision.HIGHEST, preferred_element_type=jnp.float32)


def reference(embeddings, means, variances, log_weights):
    precision, scaled, offset = component_terms(means, variances, log_weights)
    block_rows = math.gcd(NROWS, 1024)
    blocks = embeddings.reshape(NROWS // block_rows, block_rows, D)

    def advance(carry, block):
        first, second, counts = carry
        squares = block * block
        scores = row_scores(block, squares, precision, scaled, offset)
        peak = jnp.max(scores, axis=1)
        total = jnp.sum(jnp.exp(scores - peak[:, None]), axis=1)
        loglik = peak + jnp.log(total)
        resp = jnp.exp(scores - loglik[:, None])
        first = first + weighted_sum(resp, block)
        second = second + weighted_sum(resp, squares)
        counts = counts + jnp.sum(resp, axis=0)
        return (first, second, counts), loglik

    start = (jnp.zeros((K, D), jnp.float32), jnp.zeros((K, D), jnp.float32), jnp.zeros((K,), jnp.float32))
    (first, second, counts), logliks = lax.scan(advance, start, blocks)
    denom = (counts + 1.0)[:, None]
    new_means = (first + means) / denom
    new_variances = (second + variances + means * means) / denom - new_means * new_means
    new_weights = counts / NROWS
    return (new_means, new_variances, new_weights, logliks.reshape(NROWS))
```

```python
import functools

import jax
import jax.numpy as jnp
from jax import lax
from jax.experimental import pallas as pl
from jax.experimental.pallas import tpu as pltpu
from jax.sharding import PartitionSpec as P

circle_log = 1.8378770664093453
MESH = pl.DeviceIdType.MESH
NX = 4
LAG = 1.6
UNIT = 2.8


def sign(v):
    return (v > 0) - (v < 0)


def canon(d, n):
    d = d % n
    return d if d <= n // 2 else d - n


def hops_on(d, n):
    out = []
    for way in (1, -1):
        if d != 0 and (d > 0) == (way > 0):
            continue
        if abs(d) == n // 2:
            continue
        new = d - way
        if abs(new) < n // 2:
            out.append((way, new, None))
        elif abs(new) == n // 2:
            out.append((way, n // 2, 0 if way > 0 else 1))
    return out


def axes_of(stream):
    return ("x", "z") if stream == 0 else ("z", "x")


def gather_sends(stream, df, ds, nf, ns):
    first, second = axes_of(stream)
    out = []
    if ds == 0:
        out += [(first, way, (d, 0, half)) for way, d, half in hops_on(df, nf)]
    out += [(second, way, (df, d, half)) for way, d, half in hops_on(ds, ns)]
    return out


def gather_plan(nx, nz):
    size = {"x": nx, "z": nz}
    free, arrivals, plan = {}, [], []
    t = 0.0
    halves, left = {}, {(s, dx): nz for s in (0, 1) for dx in range(nx)}
    ready, dots = [], 0

    def available(stream, df, ds):
        nonlocal t
        first, second = axes_of(stream)
        for axis, way, slot in gather_sends(stream, df, ds, size[first], size[second]):
            work = (1.0 if stream == 0 else 1.125) * UNIT * (0.5 if slot[2] is not None else 1.0)
            start = max(t, free.get((axis, way), 0.0))
            free[(axis, way)] = start + work
            arrivals.append((start + work + LAG, stream, slot))
            plan.append(("send", stream, (df, ds), axis, way, slot))
        dx = (df if stream == 0 else ds) % nx
        left[(stream, dx)] -= 1
        if left[(stream, dx)] == 0:
            ready.append((stream, dx))

    available(0, 0, 0)
    available(1, 0, 0)
    plan.append(("split",))
    t += 3.0
    while arrivals or ready:
        arrivals.sort(key=lambda a: (a[0], a[1], str(a[2])))
        if arrivals and arrivals[0][0] <= t or not ready:
            when, stream, (df, ds, half) = arrivals.pop(0)
            t = max(t, when)
            plan.append(("recv", stream, (df, ds, half)))
            if half is not None:
                halves[(stream, df, ds)] = halves.get((stream, df, ds), 0) + 1
                if halves[(stream, df, ds)] < 2:
                    continue
            available(stream, df, ds)
        else:
            stream, dx = ready.pop(0)
            plan.append(("dot", stream, dx))
            t += 2.2
    return plan


def reduce_inputs(stream, df, ds, nf, ns):
    def along(d, n):
        if d == 0:
            return [(1, None), (-1, None)] if n > 2 else []
        if abs(d) == n // 2:
            return []
        far = d + sign(d)
        if abs(far) == n // 2:
            return [(n // 2, 0 if d > 0 else 1)]
        return [(far, None)]

    out = [(df, d, half) for d, half in along(ds, ns)]
    if ds == 0:
        out += [(d, 0, half) for d, half in along(df, nf)]
    return out


def reduce_sends(stream, df, ds, nf, ns):
    first, second = axes_of(stream)
    axis, d, n = (second, ds, ns) if ds != 0 else (first, df, nf)
    if d == 0:
        return []
    if abs(d) == n // 2:
        return [(axis, 1, (df, ds, 0)), (axis, -1, (df, ds, 1))]
    return [(axis, sign(d), (df, ds, None))]


def reduce_plan(nx, nz):
    size = {"x": nx, "z": nz}
    free, arrivals, plan = {}, [], []
    t = 0.0
    groups = sorted(range(nx), key=lambda dx: (-abs(canon(dx, nx)), dx))
    done, landed = set(), set()
    waiting = []
    for stream in (0, 1):
        first, second = axes_of(stream)
        for f in range(size[first]):
            for s in range(size[second]):
                waiting.append((stream, canon(f, size[first]), canon(s, size[second])))

    def is_ready(item):
        stream, df, ds = item
        first, second = axes_of(stream)
        if (df if stream == 0 else ds) % nx not in done:
            return False
        needs = reduce_inputs(stream, df, ds, size[first], size[second])
        return all((stream, n) in landed for n in needs)

    while waiting:
        for a in [a for a in arrivals if a[0] <= t]:
            arrivals.remove(a)
            landed.add(a[1:])
        ready = sorted(
            (w for w in waiting if is_ready(w)),
            key=lambda w: (-abs(w[1]) - abs(w[2]), w),
        )
        if ready:
            item = ready[0]
            waiting.remove(item)
            stream, df, ds = item
            first, second = axes_of(stream)
            plan.append(("sum", stream, (df, ds)))
            t += 0.15
            for axis, way, slot in reduce_sends(stream, df, ds, size[first], size[second]):
                work = (1.0 if stream == 0 else 1.125) * UNIT * (0.5 if slot[2] is not None else 1.0)
                start = max(t, free.get((axis, way), 0.0))
                free[(axis, way)] = start + work
                arrivals.append((start + work + LAG, stream, slot))
        elif groups:
            dx = groups.pop(0)
            plan.append(("moments", dx))
            t += 4.5
            done.add(dx)
        else:
            t = min(a[0] for a in arrivals)
    return plan


class Place:
    def __init__(self, nx, nz):
        self.nx, self.nz = nx, nz
        me = lax.axis_index("dp")
        self.x, self.z = me // nz, me % nz

    def block(self, dx, dz):
        return ((self.x + dx) % self.nx) * self.nz + (self.z + dz) % self.nz

    def of(self, stream, df, ds):
        return self.block(df, ds) if stream == 0 else self.block(ds, df)

    def group(self, dx):
        return (self.x + dx) % self.nx

    def neighbour(self, axis, way):
        dp = self.block(way, 0) if axis == "x" else self.block(0, way)
        return {"dp": dp}

    def slot(self, stream, slot):
        df, ds, half = slot
        nf, ns = (self.nx, self.nz) if stream == 0 else (self.nz, self.nx)
        return ((df % nf) * ns + ds % ns) * 2 + (half or 0)


def part(ref, index, half):
    rows = ref.shape[1]
    if half is None:
        return ref.at[index]
    return ref.at[index, pl.ds(half * (rows // 2), rows // 2)]


def greet(place, comps):
    barrier = pltpu.get_barrier_semaphore()
    count = 4
    for axis in ("x", "z"):
        for way in (1, -1):
            pl.semaphore_signal(barrier, inc=1, device_id=place.neighbour(axis, way), device_id_type=MESH)
    if comps > 1:
        mine = lax.axis_index("comp")
        for k in range(1, comps):
            pl.semaphore_signal(barrier, inc=1, device_id={"comp": (mine + k) % comps}, device_id_type=MESH)
        count += comps - 1
    pl.semaphore_wait(barrier, count)


def split(x):
    high = x.astype(jnp.bfloat16)
    return high, (x - high.astype(jnp.float32)).astype(jnp.bfloat16)


def dot_nt(a, b):
    return lax.dot_general(a, b, (((1,), (1,)), ((), ())), preferred_element_type=jnp.float32)


def dot_nn(a, b):
    return jnp.dot(a, b, preferred_element_type=jnp.float32)


def split_rows(x_ref, xh, xl, qh, ql):
    rows = x_ref.shape[0]
    tile = min(64, rows)

    @pl.loop(0, rows // tile)
    def _(i):
        at = pl.ds(pl.multiple_of(i * tile, tile), tile)
        x = x_ref[at, :]
        xh[at, :], xl[at, :] = split(x)
        qh[at, :], ql[at, :] = split(x * x)


def scores_kernel(
    nx, nz, comps, x_ref, means_ref, var_ref, logw_ref, scores_ref, norm_ref,
    scaled, prec, xh, xl, qh, ql, ph, plo, stat, send_a, recv_a, send_b, recv_b, stat_send, stat_recv,
):
    place = Place(nx, nz)
    rows, width = x_ref.shape
    size = means_ref.shape[0]
    group = nz * size
    own = place.block(0, 0)
    variances = var_ref[...]
    means = means_ref[...]
    p = 1.0 / variances
    sc = means * p
    offset = (
        logw_ref[...]
        - 0.5 * jnp.sum(jnp.log(variances), axis=1, keepdims=True)
        - 0.5 * jnp.sum(means * sc, axis=1, keepdims=True)
    )
    scaled[own] = sc
    prec[own, :, 0:width] = -0.5 * (p - 1.0)
    prec[own, :, width : width + 128] = jnp.broadcast_to(offset, (size, 128))
    greet(place, comps)

    bufs, sends, recvs = (scaled, prec), (send_a, send_b), (recv_a, recv_b)
    started = []
    seen = set()
    first_stat = True
    mine = lax.axis_index("comp")
    tile = min(256, rows)

    def copy(stream, offs, axis, way, slot):
        index = place.of(stream, *offs)
        n = place.slot(stream, slot)
        ref = part(bufs[stream], index, slot[2])
        return pltpu.make_async_remote_copy(
            src_ref=ref,
            dst_ref=ref,
            send_sem=sends[stream].at[n],
            recv_sem=recvs[stream].at[n],
            device_id=place.neighbour(axis, way),
            device_id_type=MESH,
        )

    for op in gather_plan(nx, nz):
        if op[0] == "send":
            c = copy(*op[1:])
            c.start()
            started.append(c)
        elif op[0] == "recv":
            _, stream, slot = op
            copy(stream, slot[:2], "x", 1, slot).wait_recv()
        elif op[0] == "split":
            split_rows(x_ref, xh, xl, qh, ql)
        else:
            _, stream, dx = op
            g = place.group(dx)
            blocks = pl.ds(pl.multiple_of(g * nz, nz), nz)
            at = pl.ds(pl.multiple_of(g * group, group), group)
            values = bufs[stream][blocks, :, 0:width].reshape(group, width)
            ph[...], plo[...] = split(values)
            high, low = (xh, xl) if stream == 0 else (qh, ql)
            last = dx in seen
            seen.add(dx)
            start = last and first_stat
            if last:
                first_stat = False

            @pl.loop(0, rows // tile)
            def _(i):
                n = pl.ds(pl.multiple_of(i * tile, tile), tile)
                s = dot_nt(ph[...], high[n, :]) + dot_nt(ph[...], low[n, :]) + dot_nt(plo[...], high[n, :])
                if not last:
                    scores_ref[at, n] = s
                    return
                off = prec[blocks, :, width : width + 128].reshape(group, 128)[:, 0:1]
                s = s + scores_ref[at, n] + off
                scores_ref[at, n] = s
                peak = jnp.max(s, axis=0, keepdims=True)
                if start:
                    stat[mine, 0:1, n] = peak
                    stat[mine, 1:2, n] = jnp.sum(jnp.exp(s - peak), axis=0, keepdims=True)
                else:
                    before = stat[mine, 0:1, n]
                    now = jnp.maximum(before, peak)
                    stat[mine, 1:2, n] = stat[mine, 1:2, n] * jnp.exp(before - now) + jnp.sum(
                        jnp.exp(s - now), axis=0, keepdims=True
                    )
                    stat[mine, 0:1, n] = now

    for k in range(1, comps):
        c = pltpu.make_async_remote_copy(
            src_ref=stat.at[mine],
            dst_ref=stat.at[mine],
            send_sem=stat_send.at[k],
            recv_sem=stat_recv.at[k],
            device_id={"comp": (mine + k) % comps},
            device_id_type=MESH,
        )
        c.start()
        started.append(c)
    ones = jnp.ones((8, width), jnp.bfloat16)

    @pl.loop(0, rows // tile)
    def _(i):
        n = pl.ds(pl.multiple_of(i * tile, tile), tile)
        norm_ref[:, n] = 0.5 * (dot_nt(ones, qh[n, :]) + dot_nt(ones, ql[n, :]))

    for k in range(1, comps):
        source = (mine - k + comps) % comps
        pltpu.make_async_remote_copy(
            src_ref=stat.at[source],
            dst_ref=stat.at[source],
            send_sem=stat_send.at[k],
            recv_sem=stat_recv.at[k],
            device_id={"comp": source},
            device_id_type=MESH,
        ).wait_recv()
    peak = stat[0, 0:1, :]
    for c in range(1, comps):
        peak = jnp.maximum(peak, stat[c, 0:1, :])
    total = jnp.zeros_like(peak)
    for c in range(comps):
        total = total + stat[c, 1:2, :] * jnp.exp(stat[c, 0:1, :] - peak)
    norm = peak + jnp.log(total)
    norm_ref[1:2, :] = norm - norm_ref[1:2, :] - 0.5 * width * circle_log
    norm_ref[0:1, :] = norm
    for c in started:
        c.wait_send()


def moments_kernel(
    nx, nz, x_ref, scores_ref, norm_ref, first_ref, second_ref,
    xh, xl, qh, ql, rh, rl, sum_a, sum_b, land_a, land_b, send_a, recv_a, send_b, recv_b,
):
    place = Place(nx, nz)
    rows, width = x_ref.shape
    size = first_ref.shape[0]
    group = nz * size
    split_rows(x_ref, xh, xl, qh, ql)
    greet(place, 1)
    sums, lands, sends, recvs = (sum_a, sum_b), (land_a, land_b), (send_a, send_b), (recv_a, recv_b)
    started = []

    def copy(stream, axis, way, slot):
        df, ds, half = slot
        n = place.slot(stream, slot)
        return pltpu.make_async_remote_copy(
            src_ref=part(sums[stream], place.of(stream, df, ds), half),
            dst_ref=part(lands[stream], n // 2, half),
            send_sem=sends[stream].at[n],
            recv_sem=recvs[stream].at[n],
            device_id=place.neighbour(axis, way),
            device_id_type=MESH,
        )

    for op in reduce_plan(nx, nz):
        if op[0] == "moments":
            g = place.group(op[1])
            base = g * nz
            few = max(1, nz // 4)

            @pl.loop(0, nz // few)
            def _(i):
                chunk = few * size
                at = pl.ds(pl.multiple_of(g * group + i * chunk, chunk), chunk)
                here = pl.ds(pl.multiple_of(i * chunk, chunk), chunk)
                r = jnp.exp(scores_ref[at, :] - norm_ref[0:1, :])
                counts = jnp.sum(r, axis=1, keepdims=True)
                rh[here, :], rl[here, :] = split(r)
                sum_b[pl.ds(base + i * few, few), :, width : width + 128] = jnp.broadcast_to(
                    counts, (chunk, 128)
                ).reshape(few, size, 128)

            blocks = pl.ds(pl.multiple_of(base, nz), nz)
            tile = min(256, width)

            @pl.loop(0, width // tile)
            def _(i):
                d = pl.ds(pl.multiple_of(i * tile, tile), tile)
                a = dot_nn(rh[...], xh[:, d]) + dot_nn(rh[...], xl[:, d]) + dot_nn(rl[...], xh[:, d])
                sum_a[blocks, :, d] = a.reshape(nz, size, tile)
                b = dot_nn(rh[...], qh[:, d]) + dot_nn(rh[...], ql[:, d]) + dot_nn(rl[...], qh[:, d])
                sum_b[blocks, :, d] = b.reshape(nz, size, tile)
            continue
        _, stream, (df, ds) = op
        nf, ns = (nx, nz) if stream == 0 else (nz, nx)
        index = place.of(stream, df, ds)
        whole, cut = [], []
        for slot in reduce_inputs(stream, df, ds, nf, ns):
            copy(stream, "x", 1, slot).wait_recv()
            (whole if slot[2] is None else cut).append(slot)
        out = sums[stream]
        final = (df, ds) == (0, 0)
        if whole:
            v = out[index]
            for slot in whole:
                v = v + lands[stream][place.slot(stream, slot) // 2]
            if final:
                (first_ref, second_ref)[stream][...] = v
            else:
                out[index] = v
        for slot in cut:
            at = pl.ds(slot[2] * (size // 2), size // 2)
            out[index, at] = out[index, at] + lands[stream][place.slot(stream, slot) // 2, at]
        for axis, way, slot in reduce_sends(stream, df, ds, nf, ns):
            c = copy(stream, axis, way, slot)
            c.start()
            started.append(c)
    for c in started:
        c.wait_send()


def per_device(nx, nz, comps, x, means, variances, log_weights):
    rows, width = x.shape
    size = means.shape[0]
    count = nx * nz
    local = count * size
    vmem = pl.BlockSpec(memory_space=pltpu.VMEM)
    f32, bf16 = jnp.float32, jnp.bfloat16
    parts = [pltpu.VMEM((rows, width), bf16)] * 4
    sems = [pltpu.SemaphoreType.DMA((2 * count,))] * 4
    scores, norm = pl.pallas_call(
        functools.partial(scores_kernel, nx, nz, comps),
        out_shape=(jax.ShapeDtypeStruct((local, rows), f32), jax.ShapeDtypeStruct((8, rows), f32)),
        in_specs=[vmem] * 4,
        out_specs=(vmem, vmem),
        scratch_shapes=[
            pltpu.VMEM((count, size, width), f32),
            pltpu.VMEM((count, size, width + 128), f32),
            *parts,
            pltpu.VMEM((nz * size, width), bf16),
            pltpu.VMEM((nz * size, width), bf16),
            pltpu.VMEM((comps, 8, rows), f32),
            *sems,
            pltpu.SemaphoreType.DMA((comps,)),
            pltpu.SemaphoreType.DMA((comps,)),
        ],
        compiler_params=pltpu.CompilerParams(
            collective_id=0, has_side_effects=True, vmem_limit_bytes=56 << 20
        ),
        name="scores",
    )(x, means, variances, log_weights[:, None])
    first, second = pl.pallas_call(
        functools.partial(moments_kernel, nx, nz),
        out_shape=(jax.ShapeDtypeStruct((size, width), f32), jax.ShapeDtypeStruct((size, width + 128), f32)),
        in_specs=[vmem] * 3,
        out_specs=(vmem, vmem),
        scratch_shapes=[
            *parts,
            pltpu.VMEM((nz * size, rows), bf16),
            pltpu.VMEM((nz * size, rows), bf16),
            pltpu.VMEM((count, size, width), f32),
            pltpu.VMEM((count, size, width + 128), f32),
            pltpu.VMEM((count, size, width), f32),
            pltpu.VMEM((count, size, width + 128), f32),
            *sems,
        ],
        compiler_params=pltpu.CompilerParams(
            collective_id=1, has_side_effects=True, vmem_limit_bytes=56 << 20
        ),
        name="moments",
    )(x, scores, norm)
    counts = second[:, width]
    denom = (counts + 1.0)[:, None]
    new_means = (first + means) / denom
    new_variances = (second[:, :width] + variances + means * means) / denom - new_means * new_means
    new_weights = counts / (rows * count)
    return (new_means, new_variances, new_weights, norm[1])


def solution(mesh):
    count, comps = mesh.shape["dp"], mesh.shape["comp"]
    return jax.shard_map(
        functools.partial(per_device, NX, count // NX, comps),
        mesh=mesh,
        in_specs=(
            P("dp", None),
            P(("comp", "dp"), None),
            P(("comp", "dp"), None),
            P(("comp", "dp")),
        ),
        out_specs=(P(("comp", "dp"), None), P(("comp", "dp"), None), P(("comp", "dp")), P("dp")),
        check_vma=False,
    )
```

```python
import functools

import jax
import jax.numpy as jnp
from jax import lax
from jax.experimental import pallas as pl
from jax.experimental.pallas import tpu as pltpu
from jax.sharding import PartitionSpec as P

circle_log = 1.8378770664093453
MESH = pl.DeviceIdType.MESH
NX = 4
LAG = 1.6
UNIT = 2.8
PAD = 128
IN_STREAMS = ((0, 0.0, 1.0, False), (1, 0.0, 2.0, False))
OUT_STREAMS = ((0, 0.0, 1.0, False), (1, 0.0, 2.0, False))


def columns(stream, width):
    _, lo, hi, _ = stream
    return int(lo * width), width + PAD if hi > 1.0 else int(hi * width)


def weight(stream):
    lo, hi = columns(stream, 1024)
    return (hi - lo) / 1024 * UNIT


def sign(v):
    return (v > 0) - (v < 0)


def canon(d, n):
    d = d % n
    return d if d <= n // 2 else d - n


def hops_on(d, n):
    out = []
    for way in (1, -1):
        if d != 0 and (d > 0) == (way > 0):
            continue
        if abs(d) == n // 2:
            continue
        new = d - way
        if abs(new) < n // 2:
            out.append((way, new, None))
        elif abs(new) == n // 2:
            out.append((way, n // 2, 0 if way > 0 else 1))
    return out


def axes_of(stream):
    return ("x", "z") if stream[3] else ("z", "x")


def gather_sends(stream, df, ds, nf, ns):
    first, second = axes_of(stream)
    out = []
    if ds == 0:
        out += [(first, way, (d, 0, half)) for way, d, half in hops_on(df, nf)]
    out += [(second, way, (df, d, half)) for way, d, half in hops_on(ds, ns)]
    return out


def gather_plan(nx, nz, ny):
    size = {"x": nx, "z": nz}
    free, arrivals, plan = {}, [], []
    t = 0.0
    halves = {}
    left = {(b, dx): nz * sum(s[0] == b for s in IN_STREAMS) for b in (0, 1) for dx in range(nx)}
    rows_left = 4 * ny
    whole, dots = [], []

    def push(axis, way, work, event):
        start = max(t, free.get((axis, way), 0.0))
        free[(axis, way)] = start + work
        arrivals.append((start + work + LAG, str(event), event))

    def available(k, df, ds):
        stream = IN_STREAMS[k]
        first, second = axes_of(stream)
        for axis, way, slot in gather_sends(stream, df, ds, size[first], size[second]):
            work = weight(stream) * (0.5 if slot[2] is not None else 1.0) * (2 if axis == "z" else 1)
            push(axis, way, work, ("recv", k, slot))
            plan.append(("send", k, (df, ds), axis, way, slot))
        dx = (df if stream[3] else ds) % nx
        left[(stream[0], dx)] -= 1
        if left[(stream[0], dx)] == 0:
            whole.append((stream[0], dx))
            dots.append((stream[0], dx, 0))
            if rows_left == 0:
                dots.append((stream[0], dx, 1))

    def rows_on(dy, q):
        for way, new, half in hops_on(dy, ny):
            if half is None or half == q:
                push("y", way, 2 * UNIT, ("rows", "y", new, q))
                plan.append(("rows_send", "y", way, dy, new, q))
        push("c", 1, UNIT / 3, ("rows", "c", dy, q))
        plan.append(("rows_send", "c", 0, dy, dy, q))

    for k in range(len(IN_STREAMS)):
        available(k, 0, 0)
    for q in (0, 1):
        push("z", 1, 2 * UNIT, ("rows", "p", 0, q))
        plan.append(("rows_send", "p", 0, 0, 0, q))
    plan.append(("split",))
    t += 2.5
    while arrivals or dots:
        arrivals.sort(key=lambda a: a[:2])
        if arrivals and arrivals[0][0] <= t or not dots:
            when, _, event = arrivals.pop(0)
            t = max(t, when)
            plan.append(event)
            if event[0] == "rows":
                if event[1] != "c":
                    rows_on(*event[2:])
                plan.append(("rows_split",) + event[1:])
                t += 0.2
                rows_left -= 1
                if rows_left == 0:
                    dots += [w + (1,) for w in whole]
                continue
            _, k, (df, ds, half) = event
            if half is not None:
                halves[(k, df, ds)] = halves.get((k, df, ds), 0) + 1
                if halves[(k, df, ds)] < 2:
                    continue
            available(k, df, ds)
        else:
            plan.append(("dot",) + dots.pop(0))
            t += 1.4
    return plan


def reduce_inputs(stream, df, ds, nf, ns):
    def along(d, n):
        if d == 0:
            return [(1, None), (-1, None)] if n > 2 else [(1, 0), (1, 1)]
        if abs(d) == n // 2:
            return []
        far = d + sign(d)
        if abs(far) == n // 2:
            return [(n // 2, 0 if d > 0 else 1)]
        return [(far, None)]

    out = [(df, d, half) for d, half in along(ds, ns)]
    if ds == 0:
        out += [(d, 0, half) for d, half in along(df, nf)]
    return out


def reduce_sends(stream, df, ds, nf, ns):
    first, second = axes_of(stream)
    axis, d, n = (second, ds, ns) if ds != 0 else (first, df, nf)
    if d == 0:
        return []
    if abs(d) == n // 2:
        return [(axis, 1, (df, ds, 0)), (axis, -1, (df, ds, 1))]
    return [(axis, sign(d), (df, ds, None))]


def reduce_plan(nx, nz):
    size = {"x": nx, "z": nz}
    free, arrivals, plan = {}, [], []
    t = 0.0
    groups = sorted(range(nx), key=lambda dx: (-abs(canon(dx, nx)), dx))
    done, landed = set(), set()
    waiting = []
    for k, stream in enumerate(OUT_STREAMS):
        first, second = axes_of(stream)
        for f in range(size[first]):
            for s in range(size[second]):
                waiting.append((k, canon(f, size[first]), canon(s, size[second])))

    def is_ready(item):
        k, df, ds = item
        stream = OUT_STREAMS[k]
        first, second = axes_of(stream)
        if (df if stream[3] else ds) % nx not in done:
            return False
        needs = reduce_inputs(stream, df, ds, size[first], size[second])
        return all((k, n) in landed for n in needs)

    while waiting:
        for a in [a for a in arrivals if a[0] <= t]:
            arrivals.remove(a)
            landed.add(a[1:])
        ready = sorted((w for w in waiting if is_ready(w)), key=lambda w: (-abs(w[1]) - abs(w[2]), w))
        if ready:
            item = ready[0]
            waiting.remove(item)
            k, df, ds = item
            stream = OUT_STREAMS[k]
            first, second = axes_of(stream)
            plan.append(("sum", k, (df, ds)))
            t += 0.15
            for axis, way, slot in reduce_sends(stream, df, ds, size[first], size[second]):
                work = weight(stream) * (0.5 if slot[2] is not None else 1.0) * (2 if axis == "z" else 1)
                start = max(t, free.get((axis, way), 0.0))
                free[(axis, way)] = start + work
                arrivals.append((start + work + LAG, k, slot))
        elif groups:
            dx = groups.pop(0)
            plan.append(("moments", dx))
            t += 4.5
            done.add(dx)
        else:
            t = min(a[0] for a in arrivals)
    return plan


class Place:
    def __init__(self, nx, nz, comps):
        self.nx, self.nz, self.ny = nx, nz // 2, comps // 2
        me = lax.axis_index("dp")
        self.x, z = me // nz, me % nz
        self.j, self.parity = z // 2, z % 2
        self.comp = lax.axis_index("comp")
        self.y, self.core = self.comp // 2, self.comp % 2
        self.full_z = nz

    def block(self, dx, dz):
        return ((self.x + dx) % self.nx) * self.nz + (self.j + dz) % self.nz

    def of(self, stream, df, ds):
        return self.block(df, ds) if stream[3] else self.block(ds, df)

    def group(self, dx):
        return (self.x + dx) % self.nx

    def neighbour(self, axis, way):
        x, j = (self.x + way, self.j) if axis == "x" else (self.x, self.j + way)
        return {"dp": (x % self.nx) * self.full_z + 2 * (j % self.nz) + self.parity}

    def partner(self):
        return {"dp": self.x * self.full_z + 2 * self.j + 1 - self.parity}

    def row_target(self, kind, way):
        if kind == "p":
            return self.partner()
        if kind == "y":
            return {"comp": ((self.y + way) % self.ny) * 2 + self.core}
        return {"comp": self.y * 2 + 1 - self.core}

    def slot(self, k, stream, slot):
        df, ds, half = slot
        nf, ns = (self.nx, self.nz) if stream[3] else (self.nz, self.nx)
        return ((k * nf + df % nf) * ns + ds % ns) * 2 + (half or 0)


def part(ref, index, half, cols):
    rows = ref.shape[1]
    at = pl.ds(0, rows) if half is None else pl.ds(half * (rows // 2), rows // 2)
    return ref.at[index, at, pl.ds(cols[0], cols[1] - cols[0])]


def split(x):
    high = x.astype(jnp.bfloat16)
    return high, (x - high.astype(jnp.float32)).astype(jnp.bfloat16)


def dot_nt(a, b):
    return lax.dot_general(a, b, (((1,), (1,)), ((), ())), preferred_element_type=jnp.float32)


def dot_nn(a, b):
    return jnp.dot(a, b, preferred_element_type=jnp.float32)


def kernel(
    nx, nz, comps, x_ref, means_ref, var_ref, logw_ref, first_ref, second_ref, loglik_ref,
    scaled, prec, other, xh, xl, qh, ql, ph, plo, scores, stat, norm, rh, rl,
    sum_a, sum_b, land_a, land_b,
    in_send, in_recv, out_send, out_recv, row_send, row_recv, stat_send, stat_recv,
):
    place = Place(nx, nz, comps)
    nz, ny = place.nz, place.ny
    rows, width = x_ref.shape
    size = means_ref.shape[0]
    group = nz * size
    own = place.block(0, 0)
    parity, comp = place.parity, place.comp
    own_rows = pl.multiple_of(parity * rows, rows)
    other_rows = pl.multiple_of((1 - parity) * rows, rows)
    sub = rows // comps // 2
    variances = var_ref[...]
    means = means_ref[...]
    p = 1.0 / variances
    sc = means * p
    offset = (
        logw_ref[...]
        - 0.5 * jnp.sum(jnp.log(variances), axis=1, keepdims=True)
        - 0.5 * jnp.sum(means * sc, axis=1, keepdims=True)
    )
    scaled[own] = sc
    prec[own, :, 0:width] = -0.5 * (p - 1.0)
    prec[own, :, width : width + PAD] = jnp.broadcast_to(offset, (size, PAD))

    barrier = pltpu.get_barrier_semaphore()
    friends = [place.neighbour(axis, way) for axis in ("x", "z") for way in (1, -1)]
    friends += [{"comp": (comp + k) % comps} for k in range(1, comps)]
    friends += [dict(place.partner(), comp=(comp + k) % comps) for k in range(comps)]
    for friend in friends:
        pl.semaphore_signal(barrier, inc=1, device_id=friend, device_id_type=MESH)
    pl.semaphore_wait(barrier, len(friends))

    started = []

    def begin(c):
        c.start()
        started.append(c)

    def remote(src, dst, send, recv, target):
        return pltpu.make_async_remote_copy(
            src_ref=src, dst_ref=dst, send_sem=send, recv_sem=recv, device_id=target, device_id_type=MESH
        )

    bufs = (scaled, prec)

    def param_copy(k, offs, axis, way, slot):
        stream = IN_STREAMS[k]
        n = place.slot(k, stream, slot)
        ref = part(bufs[stream[0]], place.of(stream, *offs), slot[2], columns(stream, width))
        return remote(ref, ref, in_send.at[n], in_recv.at[n], place.neighbour(axis, way))

    def slice_of(kind, dy, q):
        core = 1 - place.core if kind == "c" else place.core
        return (((place.y + dy) % ny) * 2 + core) * 2 + q

    def row_sem(kind, new, q):
        return ((("p", "y", "c").index(kind)) * ny + new % ny) * 2 + q

    def row_copy(kind, way, dy, new, q):
        index = slice_of("p", dy, q)
        n = row_sem(kind, new, q)
        if kind == "p":
            src = x_ref.at[pl.ds(pl.multiple_of(index * sub, sub), sub), :]
        else:
            src = other.at[index]
        return remote(src, other.at[index], row_send.at[n], row_recv.at[n], place.row_target(kind, way))

    def split_into(base, x):
        at = pl.ds(base, x.shape[0])
        xh[at, :], xl[at, :] = split(x)
        qh[at, :], ql[at, :] = split(x * x)

    tile = min(256, rows)
    begun = set()
    formed = set()
    for op in gather_plan(nx, nz, ny):
        if op[0] == "send":
            begin(param_copy(*op[1:]))
        elif op[0] == "recv":
            _, k, slot = op
            param_copy(k, slot[:2], "x", 1, slot).wait_recv()
        elif op[0] == "rows_send":
            begin(row_copy(*op[1:]))
        elif op[0] == "rows":
            _, kind, dy, q = op
            ref = other.at[slice_of(kind, dy, q)]
            n = row_sem(kind, dy, q)
            remote(ref, ref, row_send.at[n], row_recv.at[n], place.partner()).wait_recv()
        elif op[0] == "rows_split":
            _, kind, dy, q = op
            index = slice_of(kind, dy, q)
            split_into(pl.multiple_of(other_rows + index * sub, sub), other[index])
        elif op[0] == "split":
            few = min(64, rows)

            @pl.loop(0, rows // few)
            def _(i):
                at = pl.multiple_of(i * few, few)
                split_into(pl.multiple_of(own_rows + at, few), x_ref[pl.ds(at, few), :])
        else:
            _, b, dx, h = op
            g = place.group(dx)
            blocks = pl.ds(pl.multiple_of(g * nz, nz), nz)
            at = pl.ds(pl.multiple_of(g * group, group), group)
            ph[...], plo[...] = split(bufs[b][blocks, :, 0:width].reshape(group, width))
            high, low = (xh, xl) if b == 0 else (qh, ql)
            last = (dx, h) in formed
            formed.add((dx, h))
            opening = last and h not in begun
            if last:
                begun.add(h)
            base = own_rows if h == 0 else other_rows

            @pl.loop(0, rows // tile)
            def _(i):
                n = pl.ds(pl.multiple_of(base + i * tile, tile), tile)
                s = dot_nt(ph[...], high[n, :]) + dot_nt(ph[...], low[n, :]) + dot_nt(plo[...], high[n, :])
                if not last:
                    scores[at, n] = s
                    return
                off = prec[blocks, :, width : width + PAD].reshape(group, PAD)[:, 0:1]
                s = s + scores[at, n] + off
                scores[at, n] = s
                peak = jnp.max(s, axis=0, keepdims=True)
                if opening:
                    norm[0:1, n] = peak
                    norm[1:2, n] = jnp.sum(jnp.exp(s - peak), axis=0, keepdims=True)
                else:
                    before = norm[0:1, n]
                    now = jnp.maximum(before, peak)
                    norm[1:2, n] = norm[1:2, n] * jnp.exp(before - now) + jnp.sum(
                        jnp.exp(s - now), axis=0, keepdims=True
                    )
                    norm[0:1, n] = now

    mine = parity * comps + comp
    stat[mine] = norm[0:2, :]
    peers = [(0, k) for k in range(1, comps)] + [(1, k) for k in range(comps)]
    for other_z, k in peers:
        target = {"comp": (comp + k) % comps}
        if other_z:
            target.update(place.partner())
        n = other_z * comps + k
        begin(remote(stat.at[mine], stat.at[mine], stat_send.at[n], stat_recv.at[n], target))
    ones = jnp.ones((8, width), jnp.bfloat16)

    @pl.loop(0, rows // tile)
    def _(i):
        n = pl.ds(pl.multiple_of(own_rows + i * tile, tile), tile)
        here = pl.ds(pl.multiple_of(i * tile, tile), tile)
        loglik_ref[:, here] = 0.5 * (dot_nt(ones, qh[n, :]) + dot_nt(ones, ql[n, :])) + 0.5 * width * circle_log

    for other_z, k in peers:
        source = ((1 - parity) if other_z else parity) * comps + (comp - k + comps) % comps
        n = other_z * comps + k
        ref = stat.at[source]
        remote(ref, ref, stat_send.at[n], stat_recv.at[n], place.partner()).wait_recv()
    peak = stat[0, 0:1, :]
    for c in range(1, 2 * comps):
        peak = jnp.maximum(peak, stat[c, 0:1, :])
    total = jnp.zeros_like(peak)
    for c in range(2 * comps):
        total = total + stat[c, 1:2, :] * jnp.exp(stat[c, 0:1, :] - peak)
    norm[0:1, :] = peak + jnp.log(total)
    loglik_ref[0:1, :] = norm[0:1, pl.ds(own_rows, rows)] - loglik_ref[0:1, :]

    sums, lands, results = (sum_a, sum_b), (land_a, land_b), (first_ref, second_ref)

    def sum_copy(k, axis, way, slot):
        stream = OUT_STREAMS[k]
        df, ds, half = slot
        b, cols = stream[0], columns(stream, width)
        n = place.slot(k, stream, slot)
        return remote(
            part(sums[b], place.of(stream, df, ds), half, cols),
            part(lands[b], landing(k, slot), half, cols),
            out_send.at[n],
            out_recv.at[n],
            place.neighbour(axis, way),
        )

    def landing(k, slot):
        return place.slot(0, OUT_STREAMS[k], slot) // 2

    for op in reduce_plan(nx, nz):
        if op[0] == "moments":
            g = place.group(op[1])
            base = g * nz

            @pl.loop(0, nz)
            def _(i):
                at = pl.ds(pl.multiple_of(g * group + i * size, size), size)
                here = pl.ds(pl.multiple_of(i * size, size), size)
                r = jnp.exp(scores[at, :] - norm[0:1, :])
                rh[here, :], rl[here, :] = split(r)
                counts = jnp.sum(r, axis=1, keepdims=True)
                sum_b[base + i, :, width : width + PAD] = jnp.broadcast_to(counts, (size, PAD))

            blocks = pl.ds(pl.multiple_of(base, nz), nz)
            cols = min(256, width)

            @pl.loop(0, width // cols)
            def _(i):
                d = pl.ds(pl.multiple_of(i * cols, cols), cols)
                a = dot_nn(rh[...], xh[:, d]) + dot_nn(rh[...], xl[:, d]) + dot_nn(rl[...], xh[:, d])
                sum_a[blocks, :, d] = a.reshape(nz, size, cols)
                b = dot_nn(rh[...], qh[:, d]) + dot_nn(rh[...], ql[:, d]) + dot_nn(rl[...], qh[:, d])
                sum_b[blocks, :, d] = b.reshape(nz, size, cols)
            continue
        _, k, (df, ds) = op
        stream = OUT_STREAMS[k]
        nf, ns = (nx, nz) if stream[3] else (nz, nx)
        index = place.of(stream, df, ds)
        whole, cut = [], []
        for slot in reduce_inputs(stream, df, ds, nf, ns):
            sum_copy(k, "x", 1, slot).wait_recv()
            (whole if slot[2] is None else cut).append(slot)
        lo, hi = columns(stream, width)
        out, land = sums[stream[0]], lands[stream[0]]
        if whole:
            v = out[index, :, lo:hi]
            for slot in whole:
                v = v + land[landing(k, slot), :, lo:hi]
            out[index, :, lo:hi] = v
        for slot in cut:
            at = pl.ds(slot[2] * (size // 2), size // 2)
            out[index, at, lo:hi] = out[index, at, lo:hi] + land[landing(k, slot), at, lo:hi]
        if (df, ds) == (0, 0):
            results[stream[0]][:, lo:hi] = out[index, :, lo:hi]
        for axis, way, slot in reduce_sends(stream, df, ds, nf, ns):
            begin(sum_copy(k, axis, way, slot))
    for c in started:
        c.wait_send()


def per_device(nx, nz, comps, x, means, variances, log_weights):
    rows, width = x.shape
    size = means.shape[0]
    count = nx * nz // 2
    group = nz // 2 * size
    vmem = pl.BlockSpec(memory_space=pltpu.VMEM)
    f32, bf16 = jnp.float32, jnp.bfloat16
    dma = pltpu.SemaphoreType.DMA
    first, second, loglik = pl.pallas_call(
        functools.partial(kernel, nx, nz, comps),
        out_shape=(
            jax.ShapeDtypeStruct((size, width), f32),
            jax.ShapeDtypeStruct((size, width + PAD), f32),
            jax.ShapeDtypeStruct((8, rows), f32),
        ),
        in_specs=[vmem] * 4,
        out_specs=(vmem, vmem, vmem),
        scratch_shapes=[
            pltpu.VMEM((count, size, width), f32),
            pltpu.VMEM((count, size, width + PAD), f32),
            pltpu.VMEM((2 * comps, rows // comps // 2, width), f32),
            *[pltpu.VMEM((2 * rows, width), bf16)] * 4,
            *[pltpu.VMEM((group, width), bf16)] * 2,
            pltpu.VMEM((count * size, 2 * rows), f32),
            pltpu.VMEM((2 * comps, 2, 2 * rows), f32),
            pltpu.VMEM((8, 2 * rows), f32),
            *[pltpu.VMEM((group, 2 * rows), bf16)] * 2,
            *[pltpu.VMEM((count, size, width), f32), pltpu.VMEM((count, size, width + PAD), f32)] * 2,
            *[dma((2 * count * len(IN_STREAMS),))] * 2,
            *[dma((2 * count * len(OUT_STREAMS),))] * 2,
            *[dma((3 * comps,))] * 2,
            *[dma((2 * comps,))] * 2,
        ],
        compiler_params=pltpu.CompilerParams(
            collective_id=0, has_side_effects=True, vmem_limit_bytes=60 << 20
        ),
        name="mixture",
    )(x, means, variances, log_weights[:, None])
    counts = second[:, width]
    denom = (counts + 1.0)[:, None]
    new_means = (first + means) / denom
    new_variances = (second[:, :width] + variances + means * means) / denom - new_means * new_means
    new_weights = counts / (rows * nx * nz)
    return (new_means, new_variances, new_weights, loglik[0])


def solution(mesh):
    count, comps = mesh.shape["dp"], mesh.shape["comp"]
    return jax.shard_map(
        functools.partial(per_device, NX, count // NX, comps),
        mesh=mesh,
        in_specs=(
            P("dp", None),
            P(("comp", "dp"), None),
            P(("comp", "dp"), None),
            P(("comp", "dp")),
        ),
        out_specs=(P(("comp", "dp"), None), P(("comp", "dp"), None), P(("comp", "dp")), P("dp")),
        check_vma=False,
    )
```

```python
import functools

import jax
import jax.numpy as jnp
from jax import lax
from jax.experimental import pallas as pl
from jax.experimental.pallas import tpu as pltpu
from jax.sharding import PartitionSpec as P

circle_log = 1.8378770664093453
MESH = pl.DeviceIdType.MESH
NX = 4
LAG = 1.6
UNIT = 2.8
PAD = 128
IN_STREAMS = ((0, 0.0, 1.0, False), (1, 0.0, 2.0, False))
OUT_STREAMS = ((0, 0.0, 1.0, False), (1, 0.0, 2.0, False))


def columns(stream, width):
    _, lo, hi, _ = stream
    return int(lo * width), width + PAD if hi > 1.0 else int(hi * width)


def weight(stream):
    lo, hi = columns(stream, 1024)
    return (hi - lo) / 1024 * UNIT


def sign(v):
    return (v > 0) - (v < 0)


def canon(d, n):
    d = d % n
    return d if d <= n // 2 else d - n


def hops_on(d, n):
    out = []
    for way in (1, -1):
        if d != 0 and (d > 0) == (way > 0):
            continue
        if abs(d) == n // 2:
            continue
        new = d - way
        if abs(new) < n // 2:
            out.append((way, new, None))
        elif abs(new) == n // 2:
            out.append((way, n // 2, 0 if way > 0 else 1))
    return out


def axes_of(stream):
    return ("x", "z") if stream[3] else ("z", "x")


def gather_sends(stream, df, ds, nf, ns):
    first, second = axes_of(stream)
    out = []
    if ds == 0:
        out += [(first, way, (d, 0, half)) for way, d, half in hops_on(df, nf)]
    out += [(second, way, (df, d, half)) for way, d, half in hops_on(ds, ns)]
    return out


def gather_plan(nx, nz, ny):
    size = {"x": nx, "z": nz}
    free, arrivals, plan = {}, [], []
    t = 0.0
    halves = {}
    left = {(b, dx): nz * sum(s[0] == b for s in IN_STREAMS) for b in (0, 1) for dx in range(nx)}
    rows_left = 4 * ny
    whole, dots = [], []

    def push(axis, way, work, event):
        start = max(t, free.get((axis, way), 0.0))
        free[(axis, way)] = start + work
        arrivals.append((start + work + LAG, str(event), event))

    def available(k, df, ds):
        stream = IN_STREAMS[k]
        first, second = axes_of(stream)
        for axis, way, slot in gather_sends(stream, df, ds, size[first], size[second]):
            work = weight(stream) * (0.5 if slot[2] is not None else 1.0) * (2 if axis == "z" else 1)
            push(axis, way, work, ("recv", k, slot))
            plan.append(("send", k, (df, ds), axis, way, slot))
        dx = (df if stream[3] else ds) % nx
        left[(stream[0], dx)] -= 1
        if left[(stream[0], dx)] == 0:
            whole.append((stream[0], dx))
            dots.append((stream[0], dx, 0))
            if rows_left == 0:
                dots.append((stream[0], dx, 1))

    def rows_on(dy, q):
        for way, new, half in hops_on(dy, ny):
            if half is None or half == q:
                push("y", way, 2 * UNIT, ("rows", "y", new, q))
                plan.append(("rows_send", "y", way, dy, new, q))
        push("c", 1, UNIT / 3, ("rows", "c", dy, q))
        plan.append(("rows_send", "c", 0, dy, dy, q))

    for k in range(len(IN_STREAMS)):
        available(k, 0, 0)
    for q in (0, 1):
        push("z", 1, 2 * UNIT, ("rows", "p", 0, q))
        plan.append(("rows_send", "p", 0, 0, 0, q))
    plan.append(("split",))
    t += 2.5
    while arrivals or dots:
        arrivals.sort(key=lambda a: a[:2])
        if arrivals and arrivals[0][0] <= t or not dots:
            when, _, event = arrivals.pop(0)
            t = max(t, when)
            plan.append(event)
            if event[0] == "rows":
                if event[1] != "c":
                    rows_on(*event[2:])
                plan.append(("rows_split",) + event[1:])
                t += 0.2
                rows_left -= 1
                if rows_left == 0:
                    dots += [w + (1,) for w in whole]
                continue
            _, k, (df, ds, half) = event
            if half is not None:
                halves[(k, df, ds)] = halves.get((k, df, ds), 0) + 1
                if halves[(k, df, ds)] < 2:
                    continue
            available(k, df, ds)
        else:
            plan.append(("dot",) + dots.pop(0))
            t += 1.4
    return plan


def reduce_inputs(stream, df, ds, nf, ns):
    def along(d, n):
        if d == 0:
            return [(1, None), (-1, None)] if n > 2 else [(1, 0), (1, 1)]
        if abs(d) == n // 2:
            return []
        far = d + sign(d)
        if abs(far) == n // 2:
            return [(n // 2, 0 if d > 0 else 1)]
        return [(far, None)]

    out = [(df, d, half) for d, half in along(ds, ns)]
    if ds == 0:
        out += [(d, 0, half) for d, half in along(df, nf)]
    return out


def reduce_sends(stream, df, ds, nf, ns):
    first, second = axes_of(stream)
    axis, d, n = (second, ds, ns) if ds != 0 else (first, df, nf)
    if d == 0:
        return []
    if abs(d) == n // 2:
        return [(axis, 1, (df, ds, 0)), (axis, -1, (df, ds, 1))]
    return [(axis, sign(d), (df, ds, None))]


def reduce_plan(nx, nz):
    size = {"x": nx, "z": nz}
    free, arrivals, plan = {}, [], []
    t = 0.0
    groups = sorted(range(nx), key=lambda dx: (-abs(canon(dx, nx)), dx))
    done, landed = set(), set()
    waiting = []
    for k, stream in enumerate(OUT_STREAMS):
        first, second = axes_of(stream)
        for f in range(size[first]):
            for s in range(size[second]):
                waiting.append((k, canon(f, size[first]), canon(s, size[second])))

    def is_ready(item):
        k, df, ds = item
        stream = OUT_STREAMS[k]
        first, second = axes_of(stream)
        if (df if stream[3] else ds) % nx not in done:
            return False
        needs = reduce_inputs(stream, df, ds, size[first], size[second])
        return all((k, n) in landed for n in needs)

    while waiting:
        for a in [a for a in arrivals if a[0] <= t]:
            arrivals.remove(a)
            landed.add(a[1:])
        ready = sorted((w for w in waiting if is_ready(w)), key=lambda w: (-abs(w[1]) - abs(w[2]), w))
        if ready:
            item = ready[0]
            waiting.remove(item)
            k, df, ds = item
            stream = OUT_STREAMS[k]
            first, second = axes_of(stream)
            plan.append(("sum", k, (df, ds)))
            t += 0.15
            for axis, way, slot in reduce_sends(stream, df, ds, size[first], size[second]):
                work = weight(stream) * (0.5 if slot[2] is not None else 1.0) * (2 if axis == "z" else 1)
                start = max(t, free.get((axis, way), 0.0))
                free[(axis, way)] = start + work
                arrivals.append((start + work + LAG, k, slot))
        elif groups:
            dx = groups.pop(0)
            plan.append(("moments", dx))
            t += 4.5
            done.add(dx)
        else:
            t = min(a[0] for a in arrivals)
    return plan


class Place:
    def __init__(self, nx, nz, comps):
        self.nx, self.nz, self.ny = nx, nz // 2, comps // 2
        me = lax.axis_index("dp")
        self.x, z = me // nz, me % nz
        self.j, self.parity = z // 2, z % 2
        self.comp = lax.axis_index("comp")
        self.y, self.core = self.comp // 2, self.comp % 2
        self.full_z = nz

    def block(self, dx, dz):
        return ((self.x + dx) % self.nx) * self.nz + (self.j + dz) % self.nz

    def of(self, stream, df, ds):
        return self.block(df, ds) if stream[3] else self.block(ds, df)

    def group(self, dx):
        return (self.x + dx) % self.nx

    def neighbour(self, axis, way):
        x, j = (self.x + way, self.j) if axis == "x" else (self.x, self.j + way)
        return {"dp": (x % self.nx) * self.full_z + 2 * (j % self.nz) + self.parity}

    def partner(self):
        return {"dp": self.x * self.full_z + 2 * self.j + 1 - self.parity}

    def row_target(self, kind, way):
        if kind == "p":
            return self.partner()
        if kind == "y":
            return {"comp": ((self.y + way) % self.ny) * 2 + self.core}
        return {"comp": self.y * 2 + 1 - self.core}

    def slot(self, k, stream, slot):
        df, ds, half = slot
        nf, ns = (self.nx, self.nz) if stream[3] else (self.nz, self.nx)
        return ((k * nf + df % nf) * ns + ds % ns) * 2 + (half or 0)


def part(ref, index, half, cols):
    rows = ref.shape[1]
    at = pl.ds(0, rows) if half is None else pl.ds(half * (rows // 2), rows // 2)
    return ref.at[index, at, pl.ds(cols[0], cols[1] - cols[0])]


def split(x):
    high = x.astype(jnp.bfloat16)
    return high, (x - high.astype(jnp.float32)).astype(jnp.bfloat16)


def dot_nt(a, b):
    return lax.dot_general(a, b, (((1,), (1,)), ((), ())), preferred_element_type=jnp.float32)


def dot_nn(a, b):
    return jnp.dot(a, b, preferred_element_type=jnp.float32)


def kernel(
    nx, nz, comps, x_hbm, means_ref, var_ref, logw_ref, first_ref, second_ref, loglik_ref,
    scaled, prec, other, x_ref, xh, xl, qh, ql, pt, scores, stat, norm, rh, rl,
    sum_a, sum_b, land_a, land_b,
    in_send, in_recv, out_send, out_recv, row_send, row_recv, stat_send, stat_recv, load_sem,
):
    place = Place(nx, nz, comps)
    nz, ny = place.nz, place.ny
    rows, width = x_ref.shape
    size = means_ref.shape[0]
    load = pltpu.make_async_copy(x_hbm, x_ref, load_sem)
    load.start()
    group = nz * size
    own = place.block(0, 0)
    parity, comp = place.parity, place.comp
    own_rows = pl.multiple_of(parity * rows, rows)
    other_rows = pl.multiple_of((1 - parity) * rows, rows)
    sub = rows // comps // 2
    variances = var_ref[...]
    means = means_ref[...]
    p = 1.0 / variances
    sc = means * p
    diagonal = lax.broadcasted_iota(jnp.int32, (size, size), 0) == lax.broadcasted_iota(jnp.int32, (size, size), 1)
    offset = (
        jnp.sum(jnp.where(diagonal, logw_ref[...], 0.0), axis=1, keepdims=True)
        - 0.5 * jnp.sum(jnp.log(variances), axis=1, keepdims=True)
        - 0.5 * jnp.sum(means * sc, axis=1, keepdims=True)
    )
    scaled[own] = sc
    prec[own, :, 0:width] = -0.5 * (p - 1.0)
    prec[own, :, width : width + PAD] = jnp.broadcast_to(offset, (size, PAD))

    barrier = pltpu.get_barrier_semaphore()
    friends = [place.neighbour(axis, way) for axis in ("x", "z") for way in (1, -1)]
    friends += [{"comp": (comp + k) % comps} for k in range(1, comps)]
    friends += [dict(place.partner(), comp=(comp + k) % comps) for k in range(comps)]
    for friend in friends:
        pl.semaphore_signal(barrier, inc=1, device_id=friend, device_id_type=MESH)
    pl.semaphore_wait(barrier, len(friends))
    load.wait()

    started = []

    def begin(c):
        c.start()
        started.append(c)

    def remote(src, dst, send, recv, target):
        return pltpu.make_async_remote_copy(
            src_ref=src, dst_ref=dst, send_sem=send, recv_sem=recv, device_id=target, device_id_type=MESH
        )

    bufs = (scaled, prec)

    def param_copy(k, offs, axis, way, slot):
        stream = IN_STREAMS[k]
        n = place.slot(k, stream, slot)
        ref = part(bufs[stream[0]], place.of(stream, *offs), slot[2], columns(stream, width))
        return remote(ref, ref, in_send.at[n], in_recv.at[n], place.neighbour(axis, way))

    def slice_of(kind, dy, q):
        core = 1 - place.core if kind == "c" else place.core
        return (((place.y + dy) % ny) * 2 + core) * 2 + q

    def row_sem(kind, new, q):
        return ((("p", "y", "c").index(kind)) * ny + new % ny) * 2 + q

    def row_copy(kind, way, dy, new, q):
        index = slice_of("p", dy, q)
        n = row_sem(kind, new, q)
        if kind == "p":
            src = x_ref.at[pl.ds(pl.multiple_of(index * sub, sub), sub), :]
        else:
            src = other.at[index]
        return remote(src, other.at[index], row_send.at[n], row_recv.at[n], place.row_target(kind, way))

    def split_into(base, x):
        at = pl.ds(base, x.shape[0])
        xh[at, :], xl[at, :] = split(x)
        qh[at, :], ql[at, :] = split(x * x)

    tile = min(512, rows)
    ones = jnp.ones((8, width), jnp.bfloat16)
    begun = set()
    formed = set()
    for op in gather_plan(nx, nz, ny):
        if op[0] == "send":
            begin(param_copy(*op[1:]))
        elif op[0] == "recv":
            _, k, slot = op
            param_copy(k, slot[:2], "x", 1, slot).wait_recv()
        elif op[0] == "rows_send":
            begin(row_copy(*op[1:]))
        elif op[0] == "rows":
            _, kind, dy, q = op
            ref = other.at[slice_of(kind, dy, q)]
            n = row_sem(kind, dy, q)
            remote(ref, ref, row_send.at[n], row_recv.at[n], place.partner()).wait_recv()
        elif op[0] == "rows_split":
            _, kind, dy, q = op
            index = slice_of(kind, dy, q)
            split_into(pl.multiple_of(other_rows + index * sub, sub), other[index])
        elif op[0] == "split":
            few = min(64, rows)

            @pl.loop(0, rows // few)
            def _(i):
                at = pl.multiple_of(i * few, few)
                split_into(pl.multiple_of(own_rows + at, few), x_ref[pl.ds(at, few), :])

            few = min(256, rows)

            @pl.loop(0, rows // few)
            def _(i):
                n = pl.ds(pl.multiple_of(own_rows + i * few, few), few)
                here = pl.ds(pl.multiple_of(i * few, few), few)
                square = dot_nt(ones, qh[n, :]) + dot_nt(ones, ql[n, :])
                loglik_ref[:, here] = 0.5 * square + 0.5 * width * circle_log
        else:
            _, b, dx, h = op
            g = place.group(dx)
            blocks = pl.ds(pl.multiple_of(g * nz, nz), nz)
            at = pl.ds(pl.multiple_of(g * group, group), group)
            turned = bufs[b][blocks, :, 0:width].reshape(group, width).T
            pt[:, 0:group], pt[:, group : 2 * group] = split(turned)
            high, low = (xh, xl) if b == 0 else (qh, ql)
            last = (dx, h) in formed
            formed.add((dx, h))
            opening = last and h not in begun
            if last:
                begun.add(h)
            base = own_rows if h == 0 else other_rows

            @pl.loop(0, rows // tile)
            def _(i):
                n = pl.ds(pl.multiple_of(base + i * tile, tile), tile)
                both = dot_nn(high[n, :], pt[...])
                s = both[:, 0:group] + both[:, group : 2 * group] + dot_nn(low[n, :], pt[:, 0:group])
                s = s.T
                if not last:
                    scores[at, n] = s
                    return
                off = prec[blocks, :, width : width + PAD].reshape(group, PAD)[:, 0:1]
                s = s + scores[at, n] + off
                scores[at, n] = s
                peak = jnp.max(s, axis=0, keepdims=True)
                if opening:
                    norm[0:1, n] = peak
                    norm[1:2, n] = jnp.sum(jnp.exp(s - peak), axis=0, keepdims=True)
                else:
                    before = norm[0:1, n]
                    now = jnp.maximum(before, peak)
                    norm[1:2, n] = norm[1:2, n] * jnp.exp(before - now) + jnp.sum(
                        jnp.exp(s - now), axis=0, keepdims=True
                    )
                    norm[0:1, n] = now

    mine = parity * comps + comp
    stat[mine] = norm[0:2, :]
    peers = [(0, k) for k in range(1, comps)] + [(1, k) for k in range(comps)]
    for other_z, k in peers:
        target = {"comp": (comp + k) % comps}
        if other_z:
            target.update(place.partner())
        n = other_z * comps + k
        begin(remote(stat.at[mine], stat.at[mine], stat_send.at[n], stat_recv.at[n], target))

    for other_z, k in peers:
        source = ((1 - parity) if other_z else parity) * comps + (comp - k + comps) % comps
        n = other_z * comps + k
        ref = stat.at[source]
        remote(ref, ref, stat_send.at[n], stat_recv.at[n], place.partner()).wait_recv()
    peak = stat[0, 0:1, :]
    for c in range(1, 2 * comps):
        peak = jnp.maximum(peak, stat[c, 0:1, :])
    total = jnp.zeros_like(peak)
    for c in range(2 * comps):
        total = total + stat[c, 1:2, :] * jnp.exp(stat[c, 0:1, :] - peak)
    norm[0:1, :] = peak + jnp.log(total)
    loglik_ref[0:1, :] = norm[0:1, pl.ds(own_rows, rows)] - loglik_ref[0:1, :]

    sums, lands, results = (sum_a, sum_b), (land_a, land_b), (first_ref, second_ref)

    def sum_copy(k, axis, way, slot):
        stream = OUT_STREAMS[k]
        df, ds, half = slot
        b, cols = stream[0], columns(stream, width)
        n = place.slot(k, stream, slot)
        return remote(
            part(sums[b], place.of(stream, df, ds), half, cols),
            part(lands[b], landing(k, slot), half, cols),
            out_send.at[n],
            out_recv.at[n],
            place.neighbour(axis, way),
        )

    def landing(k, slot):
        return place.slot(0, OUT_STREAMS[k], slot) // 2

    for op in reduce_plan(nx, nz):
        if op[0] == "moments":
            g = place.group(op[1])
            base = g * nz

            @pl.loop(0, nz)
            def _(i):
                at = pl.ds(pl.multiple_of(g * group + i * size, size), size)
                here = pl.ds(pl.multiple_of(i * size, size), size)
                r = jnp.exp(scores[at, :] - norm[0:1, :])
                rh[here, :], rl[here, :] = split(r)
                counts = jnp.sum(r, axis=1, keepdims=True)
                sum_b[base + i, :, width : width + PAD] = jnp.broadcast_to(counts, (size, PAD))

            blocks = pl.ds(pl.multiple_of(base, nz), nz)
            cols = min(256, width)

            @pl.loop(0, width // cols)
            def _(i):
                d = pl.ds(pl.multiple_of(i * cols, cols), cols)
                a = dot_nn(rh[...], xh[:, d]) + dot_nn(rh[...], xl[:, d]) + dot_nn(rl[...], xh[:, d])
                sum_a[blocks, :, d] = a.reshape(nz, size, cols)
                b = dot_nn(rh[...], qh[:, d]) + dot_nn(rh[...], ql[:, d]) + dot_nn(rl[...], qh[:, d])
                sum_b[blocks, :, d] = b.reshape(nz, size, cols)
            continue
        _, k, (df, ds) = op
        stream = OUT_STREAMS[k]
        nf, ns = (nx, nz) if stream[3] else (nz, nx)
        index = place.of(stream, df, ds)
        whole, cut = [], []
        for slot in reduce_inputs(stream, df, ds, nf, ns):
            sum_copy(k, "x", 1, slot).wait_recv()
            (whole if slot[2] is None else cut).append(slot)
        lo, hi = columns(stream, width)
        out, land = sums[stream[0]], lands[stream[0]]
        if whole:
            v = out[index, :, lo:hi]
            for slot in whole:
                v = v + land[landing(k, slot), :, lo:hi]
            out[index, :, lo:hi] = v
        for slot in cut:
            at = pl.ds(slot[2] * (size // 2), size // 2)
            out[index, at, lo:hi] = out[index, at, lo:hi] + land[landing(k, slot), at, lo:hi]
        if (df, ds) == (0, 0):
            results[stream[0]][:, lo:hi] = out[index, :, lo:hi]
        for axis, way, slot in reduce_sends(stream, df, ds, nf, ns):
            begin(sum_copy(k, axis, way, slot))
    for c in started:
        c.wait_send()


def per_device(nx, nz, comps, x, means, variances, log_weights):
    rows, width = x.shape
    size = means.shape[0]
    count = nx * nz // 2
    group = nz // 2 * size
    vmem = pl.BlockSpec(memory_space=pltpu.VMEM)
    f32, bf16 = jnp.float32, jnp.bfloat16
    dma = pltpu.SemaphoreType.DMA
    first, second, loglik = pl.pallas_call(
        functools.partial(kernel, nx, nz, comps),
        out_shape=(
            jax.ShapeDtypeStruct((size, width), f32),
            jax.ShapeDtypeStruct((size, width + PAD), f32),
            jax.ShapeDtypeStruct((8, rows), f32),
        ),
        in_specs=[pl.BlockSpec(memory_space=pl.ANY)] + [vmem] * 3,
        out_specs=(vmem, vmem, vmem),
        scratch_shapes=[
            pltpu.VMEM((count, size, width), f32),
            pltpu.VMEM((count, size, width + PAD), f32),
            pltpu.VMEM((2 * comps, rows // comps // 2, width), f32),
            pltpu.VMEM((rows, width), f32),
            *[pltpu.VMEM((2 * rows, width), bf16)] * 4,
            pltpu.VMEM((width, 2 * group), bf16),
            pltpu.VMEM((count * size, 2 * rows), f32),
            pltpu.VMEM((2 * comps, 2, 2 * rows), f32),
            pltpu.VMEM((8, 2 * rows), f32),
            *[pltpu.VMEM((group, 2 * rows), bf16)] * 2,
            *[pltpu.VMEM((count, size, width), f32), pltpu.VMEM((count, size, width + PAD), f32)] * 2,
            *[dma((2 * count * len(IN_STREAMS),))] * 2,
            *[dma((2 * count * len(OUT_STREAMS),))] * 2,
            *[dma((3 * comps,))] * 2,
            *[dma((2 * comps,))] * 2,
            dma,
        ],
        compiler_params=pltpu.CompilerParams(
            collective_id=0, has_side_effects=True, vmem_limit_bytes=60 << 20
        ),
        name="mixture",
    )(x, means, variances, log_weights[None, :])
    counts = second[:, width]
    denom = (counts + 1.0)[:, None]
    new_means = (first + means) / denom
    new_variances = (second[:, :width] + variances + means * means) / denom - new_means * new_means
    new_weights = counts / (rows * nx * nz)
    return (new_means, new_variances, new_weights, loglik[0])


def solution(mesh):
    count, comps = mesh.shape["dp"], mesh.shape["comp"]
    return jax.shard_map(
        functools.partial(per_device, NX, count // NX, comps),
        mesh=mesh,
        in_specs=(
            P("dp", None),
            P(("comp", "dp"), None),
            P(("comp", "dp"), None),
            P(("comp", "dp")),
        ),
        out_specs=(P(("comp", "dp"), None), P(("comp", "dp"), None), P(("comp", "dp")), P("dp")),
        check_vma=False,
    )
```

```python
import functools

import jax
import jax.numpy as jnp
from jax import lax
from jax.experimental import pallas as pl
from jax.experimental.pallas import tpu as pltpu
from jax.sharding import PartitionSpec as P

circle_log = 1.8378770664093453
MESH = pl.DeviceIdType.MESH
NX = 4
LAG = 1.6
UNIT = 2.8
PAD = 128
IN_STREAMS = ((0, 0.0, 1.0, False), (1, 0.0, 2.0, False))
OUT_STREAMS = ((0, 0.0, 1.0, False), (1, 0.0, 2.0, False))


def columns(stream, width):
    _, lo, hi, _ = stream
    return int(lo * width), width + PAD if hi > 1.0 else int(hi * width)


def weight(stream):
    lo, hi = columns(stream, 1024)
    return (hi - lo) / 1024 * UNIT


def sign(v):
    return (v > 0) - (v < 0)


def canon(d, n):
    d = d % n
    return d if d <= n // 2 else d - n


def hops_on(d, n):
    out = []
    for way in (1, -1):
        if d != 0 and (d > 0) == (way > 0):
            continue
        if abs(d) == n // 2:
            continue
        new = d - way
        if abs(new) < n // 2:
            out.append((way, new, None))
        elif abs(new) == n // 2:
            out.append((way, n // 2, 0 if way > 0 else 1))
    return out


def axes_of(stream):
    return ("x", "z") if stream[3] else ("z", "x")


def gather_sends(stream, df, ds, nf, ns):
    first, second = axes_of(stream)
    out = []
    if ds == 0:
        out += [(first, way, (d, 0, half)) for way, d, half in hops_on(df, nf)]
    out += [(second, way, (df, d, half)) for way, d, half in hops_on(ds, ns)]
    return out


def gather_plan(nx, nz, ny):
    size = {"x": nx, "z": nz}
    free, arrivals, plan = {}, [], []
    t = 0.0
    halves = {}
    left = {(b, dx): nz * sum(s[0] == b for s in IN_STREAMS) for b in (0, 1) for dx in range(nx)}
    rows_left = {canon(y, ny): 4 for y in range(ny)}
    whole, dots, here = [], [], []

    def push(axis, way, work, event):
        start = max(t, free.get((axis, way), 0.0))
        free[(axis, way)] = start + work
        arrivals.append((start + work + LAG, str(event), event))

    def available(k, df, ds):
        stream = IN_STREAMS[k]
        first, second = axes_of(stream)
        for axis, way, slot in gather_sends(stream, df, ds, size[first], size[second]):
            work = weight(stream) * (0.5 if slot[2] is not None else 1.0) * (2 if axis == "z" else 1)
            push(axis, way, work, ("recv", k, slot))
            plan.append(("send", k, (df, ds), axis, way, slot))
        dx = (df if stream[3] else ds) % nx
        left[(stream[0], dx)] -= 1
        if left[(stream[0], dx)] == 0:
            whole.append((stream[0], dx))
            dots.append(("turn", stream[0], dx))
            dots.extend(("dot", stream[0], dx, c) for c in here)

    def rows_on(dy, q):
        for way, new, half in hops_on(dy, ny):
            if half is None or half == q:
                push("y", way, 2 * UNIT, ("rows", "y", new, q))
                plan.append(("rows_send", "y", way, dy, new, q))
        push("c", 1, UNIT / 3, ("rows", "c", dy, q))
        plan.append(("rows_send", "c", 0, dy, dy, q))

    def rows_here(chunk):
        here.append(chunk)
        dots.extend(("dot",) + w + (chunk,) for w in whole)

    def rows_go(q):
        push("z", 1, 2 * UNIT, ("rows", "p", 0, q))
        plan.append(("rows_send", "p", 0, 0, 0, q))

    def rows_after(k, d):
        relays.discard((k, d))
        if not relays and rows_sent == []:
            for q in (0, 1):
                rows_go(q)
                rows_sent.append(q)

    rows_sent = []
    relays = {(k, d) for k in range(len(IN_STREAMS)) for d in ((-1, 1) if nz > 2 else (0,))}
    for k in range(len(IN_STREAMS)):
        available(k, 0, 0)
        rows_after(k, 0)
    plan.append(("split",))
    t += 4.0
    rows_here(None)
    while arrivals or dots:
        arrivals.sort(key=lambda a: a[:2])
        if arrivals and arrivals[0][0] <= t or not dots:
            when, _, event = arrivals.pop(0)
            t = max(t, when)
            plan.append(event)
            if event[0] == "rows":
                if event[1] != "c":
                    rows_on(*event[2:])
                plan.append(("rows_split",) + event[1:])
                t += 0.2
                rows_left[event[2]] -= 1
                if rows_left[event[2]] == 0:
                    rows_here(event[2])
                continue
            _, k, (df, ds, half) = event
            if half is not None:
                halves[(k, df, ds)] = halves.get((k, df, ds), 0) + 1
                if halves[(k, df, ds)] < 2:
                    continue
            available(k, df, ds)
            if ds == 0:
                rows_after(k, df)
        else:
            op = dots.pop(0)
            plan.append(op)
            t += 0.3 if op[0] == "turn" else 1.6 if op[3] is None else 0.45
    return plan


def reduce_inputs(stream, df, ds, nf, ns):
    def along(d, n):
        if d == 0:
            return [(1, None), (-1, None)] if n > 2 else [(1, 0), (1, 1)]
        if abs(d) == n // 2:
            return []
        far = d + sign(d)
        if abs(far) == n // 2:
            return [(n // 2, 0 if d > 0 else 1)]
        return [(far, None)]

    out = [(df, d, half) for d, half in along(ds, ns)]
    if ds == 0:
        out += [(d, 0, half) for d, half in along(df, nf)]
    return out


def reduce_sends(stream, df, ds, nf, ns):
    first, second = axes_of(stream)
    axis, d, n = (second, ds, ns) if ds != 0 else (first, df, nf)
    if d == 0:
        return []
    if abs(d) == n // 2:
        return [(axis, 1, (df, ds, 0)), (axis, -1, (df, ds, 1))]
    return [(axis, sign(d), (df, ds, None))]


def reduce_plan(nx, nz):
    size = {"x": nx, "z": nz}
    free, arrivals, plan = {}, [], []
    t = 0.0
    groups = sorted(range(nx), key=lambda dx: (-abs(canon(dx, nx)), dx))
    done, landed = set(), set()
    waiting = []
    for k, stream in enumerate(OUT_STREAMS):
        first, second = axes_of(stream)
        for f in range(size[first]):
            for s in range(size[second]):
                waiting.append((k, canon(f, size[first]), canon(s, size[second])))

    def is_ready(item):
        k, df, ds = item
        stream = OUT_STREAMS[k]
        first, second = axes_of(stream)
        if (df if stream[3] else ds) % nx not in done:
            return False
        needs = reduce_inputs(stream, df, ds, size[first], size[second])
        return all((k, n) in landed for n in needs)

    while waiting:
        for a in [a for a in arrivals if a[0] <= t]:
            arrivals.remove(a)
            landed.add(a[1:])
        ready = sorted((w for w in waiting if is_ready(w)), key=lambda w: (-abs(w[1]) - abs(w[2]), w))
        if ready:
            item = ready[0]
            waiting.remove(item)
            k, df, ds = item
            stream = OUT_STREAMS[k]
            first, second = axes_of(stream)
            plan.append(("sum", k, (df, ds)))
            t += 0.15
            for axis, way, slot in reduce_sends(stream, df, ds, size[first], size[second]):
                work = weight(stream) * (0.5 if slot[2] is not None else 1.0) * (2 if axis == "z" else 1)
                start = max(t, free.get((axis, way), 0.0))
                free[(axis, way)] = start + work
                arrivals.append((start + work + LAG, k, slot))
        elif groups:
            dx = groups.pop(0)
            plan.append(("moments", dx))
            t += 4.5
            done.add(dx)
        else:
            t = min(a[0] for a in arrivals)
    return plan


class Place:
    def __init__(self, nx, nz, comps):
        self.nx, self.nz, self.ny = nx, nz // 2, comps // 2
        me = lax.axis_index("dp")
        self.x, z = me // nz, me % nz
        self.j, self.parity = z // 2, z % 2
        self.comp = lax.axis_index("comp")
        self.y, self.core = self.comp // 2, self.comp % 2
        self.full_z = nz

    def block(self, dx, dz):
        return ((self.x + dx) % self.nx) * self.nz + (self.j + dz) % self.nz

    def of(self, stream, df, ds):
        return self.block(df, ds) if stream[3] else self.block(ds, df)

    def group(self, dx):
        return (self.x + dx) % self.nx

    def neighbour(self, axis, way):
        x, j = (self.x + way, self.j) if axis == "x" else (self.x, self.j + way)
        return {"dp": (x % self.nx) * self.full_z + 2 * (j % self.nz) + self.parity}

    def partner(self):
        return {"dp": self.x * self.full_z + 2 * self.j + 1 - self.parity}

    def row_target(self, kind, way):
        if kind == "p":
            return self.partner()
        if kind == "y":
            return {"comp": ((self.y + way) % self.ny) * 2 + self.core}
        return {"comp": self.y * 2 + 1 - self.core}

    def slot(self, k, stream, slot):
        df, ds, half = slot
        nf, ns = (self.nx, self.nz) if stream[3] else (self.nz, self.nx)
        return ((k * nf + df % nf) * ns + ds % ns) * 2 + (half or 0)


def part(ref, index, half, cols):
    rows = ref.shape[1]
    at = pl.ds(0, rows) if half is None else pl.ds(half * (rows // 2), rows // 2)
    return ref.at[index, at, pl.ds(cols[0], cols[1] - cols[0])]


def split(x):
    high = x.astype(jnp.bfloat16)
    return high, (x - high.astype(jnp.float32)).astype(jnp.bfloat16)


def dot_nt(a, b):
    return lax.dot_general(a, b, (((1,), (1,)), ((), ())), preferred_element_type=jnp.float32)


def dot_nn(a, b):
    return jnp.dot(a, b, preferred_element_type=jnp.float32)


def kernel(
    nx, nz, comps, x_hbm, means_ref, var_ref, logw_ref, first_ref, second_ref, loglik_ref,
    scaled, prec, other, x_ref, xh, xl, qh, ql, pt, scores, stat, norm, rh, rl,
    sum_a, sum_b, land_a, land_b,
    in_send, in_recv, out_send, out_recv, row_send, row_recv, stat_send, stat_recv, load_sem,
):
    place = Place(nx, nz, comps)
    nz, ny = place.nz, place.ny
    rows, width = x_ref.shape
    size = means_ref.shape[0]
    load = pltpu.make_async_copy(x_hbm, x_ref, load_sem)
    load.start()
    group = nz * size
    own = place.block(0, 0)
    parity, comp = place.parity, place.comp
    own_rows = pl.multiple_of(parity * rows, rows)
    other_rows = pl.multiple_of((1 - parity) * rows, rows)
    sub = rows // comps // 2
    variances = var_ref[...]
    means = means_ref[...]
    p = 1.0 / variances
    sc = means * p
    diagonal = lax.broadcasted_iota(jnp.int32, (size, size), 0) == lax.broadcasted_iota(jnp.int32, (size, size), 1)
    offset = (
        jnp.sum(jnp.where(diagonal, logw_ref[...], 0.0), axis=1, keepdims=True)
        - 0.5 * jnp.sum(jnp.log(variances), axis=1, keepdims=True)
        - 0.5 * jnp.sum(means * sc, axis=1, keepdims=True)
    )
    scaled[own] = sc
    prec[own, :, 0:width] = -0.5 * (p - 1.0)
    prec[own, :, width : width + PAD] = jnp.broadcast_to(offset, (size, PAD))

    barrier = pltpu.get_barrier_semaphore()
    friends = [place.neighbour(axis, way) for axis in ("x", "z") for way in (1, -1)]
    friends += [{"comp": (comp + k) % comps} for k in range(1, comps)]
    friends += [dict(place.partner(), comp=(comp + k) % comps) for k in range(comps)]
    for friend in friends:
        pl.semaphore_signal(barrier, inc=1, device_id=friend, device_id_type=MESH)
    pl.semaphore_wait(barrier, len(friends))
    load.wait()

    started = []

    def begin(c):
        c.start()
        started.append(c)

    def remote(src, dst, send, recv, target):
        return pltpu.make_async_remote_copy(
            src_ref=src, dst_ref=dst, send_sem=send, recv_sem=recv, device_id=target, device_id_type=MESH
        )

    bufs = (scaled, prec)

    def param_copy(k, offs, axis, way, slot):
        stream = IN_STREAMS[k]
        n = place.slot(k, stream, slot)
        ref = part(bufs[stream[0]], place.of(stream, *offs), slot[2], columns(stream, width))
        return remote(ref, ref, in_send.at[n], in_recv.at[n], place.neighbour(axis, way))

    def slice_of(kind, dy, q):
        core = 1 - place.core if kind == "c" else place.core
        return (((place.y + dy) % ny) * 2 + core) * 2 + q

    def row_sem(kind, new, q):
        return ((("p", "y", "c").index(kind)) * ny + new % ny) * 2 + q

    def row_copy(kind, way, dy, new, q):
        index = slice_of("p", dy, q)
        n = row_sem(kind, new, q)
        if kind == "p":
            src = x_ref.at[pl.ds(pl.multiple_of(index * sub, sub), sub), :]
        else:
            src = other.at[index]
        return remote(src, other.at[index], row_send.at[n], row_recv.at[n], place.row_target(kind, way))

    def split_into(base, x):
        at = pl.ds(base, x.shape[0])
        xh[at, :], xl[at, :] = split(x)
        qh[at, :], ql[at, :] = split(x * x)

    ones = jnp.ones((8, width), jnp.bfloat16)
    begun = set()
    formed = set()
    for op in gather_plan(nx, nz, ny):
        if op[0] == "send":
            begin(param_copy(*op[1:]))
        elif op[0] == "recv":
            _, k, slot = op
            param_copy(k, slot[:2], "x", 1, slot).wait_recv()
        elif op[0] == "rows_send":
            begin(row_copy(*op[1:]))
        elif op[0] == "rows":
            _, kind, dy, q = op
            ref = other.at[slice_of(kind, dy, q)]
            n = row_sem(kind, dy, q)
            remote(ref, ref, row_send.at[n], row_recv.at[n], place.partner()).wait_recv()
        elif op[0] == "rows_split":
            _, kind, dy, q = op
            index = slice_of(kind, dy, q)
            split_into(pl.multiple_of(other_rows + index * sub, sub), other[index])
        elif op[0] == "split":
            few = min(64, rows)

            @pl.loop(0, rows // few)
            def _(i):
                at = pl.multiple_of(i * few, few)
                split_into(pl.multiple_of(own_rows + at, few), x_ref[pl.ds(at, few), :])

            few = min(256, rows)

            @pl.loop(0, rows // few)
            def _(i):
                n = pl.ds(pl.multiple_of(own_rows + i * few, few), few)
                here = pl.ds(pl.multiple_of(i * few, few), few)
                square = dot_nt(ones, qh[n, :]) + dot_nt(ones, ql[n, :])
                loglik_ref[:, here] = 0.5 * square[0:1, :] + 0.5 * width * circle_log
        elif op[0] == "turn":
            _, b, dx = op
            blocks = pl.ds(pl.multiple_of(place.group(dx) * nz, nz), nz)
            turned = bufs[b][blocks, :, 0:width].reshape(group, width).T
            pt[b * nx + dx, :, 0:group], pt[b * nx + dx, :, group : 2 * group] = split(turned)
        else:
            _, b, dx, h = op
            g = place.group(dx)
            blocks = pl.ds(pl.multiple_of(g * nz, nz), nz)
            at = pl.ds(pl.multiple_of(g * group, group), group)
            params = pt.at[b * nx + dx]
            high, low = (xh, xl) if b == 0 else (qh, ql)
            last = (dx, h) in formed
            formed.add((dx, h))
            opening = last and h not in begun
            if last:
                begun.add(h)
            many = 4 * sub
            base = own_rows if h is None else other_rows + ((place.y + h) % ny) * many
            count = rows if h is None else many
            tile = min(256, count)

            @pl.loop(0, count // tile)
            def _(i):
                n = pl.ds(pl.multiple_of(base + i * tile, tile), tile)
                both = dot_nn(high[n, :], params[...])
                s = both[:, 0:group] + both[:, group : 2 * group] + dot_nn(low[n, :], params[:, 0:group])
                s = s.T
                if not last:
                    scores[at, n] = s
                    return
                off = prec[blocks, :, width : width + PAD].reshape(group, PAD)[:, 0:1]
                s = s + scores[at, n] + off
                scores[at, n] = s
                peak = jnp.max(s, axis=0, keepdims=True)
                if opening:
                    norm[0:1, n] = peak
                    norm[1:2, n] = jnp.sum(jnp.exp(s - peak), axis=0, keepdims=True)
                else:
                    before = norm[0:1, n]
                    now = jnp.maximum(before, peak)
                    norm[1:2, n] = norm[1:2, n] * jnp.exp(before - now) + jnp.sum(
                        jnp.exp(s - now), axis=0, keepdims=True
                    )
                    norm[0:1, n] = now

    mine = parity * comps + comp
    stat[mine] = norm[0:2, :]
    peers = [(0, k) for k in range(1, comps)] + [(1, k) for k in range(comps)]
    for other_z, k in peers:
        target = {"comp": (comp + k) % comps}
        if other_z:
            target.update(place.partner())
        n = other_z * comps + k
        begin(remote(stat.at[mine], stat.at[mine], stat_send.at[n], stat_recv.at[n], target))

    for other_z, k in peers:
        source = ((1 - parity) if other_z else parity) * comps + (comp - k + comps) % comps
        n = other_z * comps + k
        ref = stat.at[source]
        remote(ref, ref, stat_send.at[n], stat_recv.at[n], place.partner()).wait_recv()
    peak = stat[0, 0:1, :]
    for c in range(1, 2 * comps):
        peak = jnp.maximum(peak, stat[c, 0:1, :])
    total = jnp.zeros_like(peak)
    for c in range(2 * comps):
        total = total + stat[c, 1:2, :] * jnp.exp(stat[c, 0:1, :] - peak)
    norm[0:1, :] = peak + jnp.log(total)
    loglik_ref[...] = norm[0:1, pl.ds(own_rows, rows)] - loglik_ref[...]

    sums, lands, results = (sum_a, sum_b), (land_a, land_b), (first_ref, second_ref)

    def sum_copy(k, axis, way, slot):
        stream = OUT_STREAMS[k]
        df, ds, half = slot
        b, cols = stream[0], columns(stream, width)
        n = place.slot(k, stream, slot)
        return remote(
            part(sums[b], place.of(stream, df, ds), half, cols),
            part(lands[b], landing(k, slot), half, cols),
            out_send.at[n],
            out_recv.at[n],
            place.neighbour(axis, way),
        )

    def landing(k, slot):
        return place.slot(0, OUT_STREAMS[k], slot) // 2

    for op in reduce_plan(nx, nz):
        if op[0] == "moments":
            g = place.group(op[1])
            base = g * nz

            @pl.loop(0, nz)
            def _(i):
                at = pl.ds(pl.multiple_of(g * group + i * size, size), size)
                here = pl.ds(pl.multiple_of(i * size, size), size)
                r = jnp.exp(scores[at, :] - norm[0:1, :])
                rh[here, :], rl[here, :] = split(r)
                counts = jnp.sum(r, axis=1, keepdims=True)
                sum_b[base + i, :, width : width + PAD] = jnp.broadcast_to(counts, (size, PAD))

            blocks = pl.ds(pl.multiple_of(base, nz), nz)
            cols = min(256, width)

            @pl.loop(0, width // cols)
            def _(i):
                d = pl.ds(pl.multiple_of(i * cols, cols), cols)
                a = dot_nn(rh[...], xh[:, d]) + dot_nn(rh[...], xl[:, d]) + dot_nn(rl[...], xh[:, d])
                sum_a[blocks, :, d] = a.reshape(nz, size, cols)
                b = dot_nn(rh[...], qh[:, d]) + dot_nn(rh[...], ql[:, d]) + dot_nn(rl[...], qh[:, d])
                sum_b[blocks, :, d] = b.reshape(nz, size, cols)
            continue
        _, k, (df, ds) = op
        stream = OUT_STREAMS[k]
        nf, ns = (nx, nz) if stream[3] else (nz, nx)
        index = place.of(stream, df, ds)
        whole, cut = [], []
        for slot in reduce_inputs(stream, df, ds, nf, ns):
            sum_copy(k, "x", 1, slot).wait_recv()
            (whole if slot[2] is None else cut).append(slot)
        lo, hi = columns(stream, width)
        out, land = sums[stream[0]], lands[stream[0]]
        if whole:
            v = out[index, :, lo:hi]
            for slot in whole:
                v = v + land[landing(k, slot), :, lo:hi]
            out[index, :, lo:hi] = v
        for slot in cut:
            at = pl.ds(slot[2] * (size // 2), size // 2)
            out[index, at, lo:hi] = out[index, at, lo:hi] + land[landing(k, slot), at, lo:hi]
        if (df, ds) == (0, 0):
            results[stream[0]][:, lo:hi] = out[index, :, lo:hi]
        for axis, way, slot in reduce_sends(stream, df, ds, nf, ns):
            begin(sum_copy(k, axis, way, slot))
    for c in started:
        c.wait_send()


def per_device(nx, nz, comps, x, means, variances, log_weights):
    rows, width = x.shape
    size = means.shape[0]
    count = nx * nz // 2
    group = nz // 2 * size
    vmem = pl.BlockSpec(memory_space=pltpu.VMEM)
    f32, bf16 = jnp.float32, jnp.bfloat16
    dma = pltpu.SemaphoreType.DMA
    first, second, loglik = pl.pallas_call(
        functools.partial(kernel, nx, nz, comps),
        out_shape=(
            jax.ShapeDtypeStruct((size, width), f32),
            jax.ShapeDtypeStruct((size, width + PAD), f32),
            jax.ShapeDtypeStruct((1, rows), f32),
        ),
        in_specs=[pl.BlockSpec(memory_space=pl.ANY)] + [vmem] * 3,
        out_specs=(vmem, vmem, vmem),
        scratch_shapes=[
            pltpu.VMEM((count, size, width), f32),
            pltpu.VMEM((count, size, width + PAD), f32),
            pltpu.VMEM((2 * comps, rows // comps // 2, width), f32),
            pltpu.VMEM((rows, width), f32),
            *[pltpu.VMEM((2 * rows, width), bf16)] * 4,
            pltpu.VMEM((2 * nx, width, 2 * group), bf16),
            pltpu.VMEM((count * size, 2 * rows), f32),
            pltpu.VMEM((2 * comps, 2, 2 * rows), f32),
            pltpu.VMEM((8, 2 * rows), f32),
            *[pltpu.VMEM((group, 2 * rows), bf16)] * 2,
            *[pltpu.VMEM((count, size, width), f32), pltpu.VMEM((count, size, width + PAD), f32)] * 2,
            *[dma((2 * count * len(IN_STREAMS),))] * 2,
            *[dma((2 * count * len(OUT_STREAMS),))] * 2,
            *[dma((3 * comps,))] * 2,
            *[dma((2 * comps,))] * 2,
            dma,
        ],
        compiler_params=pltpu.CompilerParams(
            collective_id=0, has_side_effects=True, vmem_limit_bytes=60 << 20
        ),
        name="mixture",
    )(x, means, variances, log_weights[None, :])
    counts = second[:, width]
    denom = (counts + 1.0)[:, None]
    new_means = (first + means) / denom
    new_variances = (second[:, :width] + variances + means * means) / denom - new_means * new_means
    new_weights = counts / (rows * nx * nz)
    return (new_means, new_variances, new_weights, loglik.reshape(rows))


def solution(mesh):
    count, comps = mesh.shape["dp"], mesh.shape["comp"]
    return jax.shard_map(
        functools.partial(per_device, NX, count // NX, comps),
        mesh=mesh,
        in_specs=(
            P("dp", None),
            P(("comp", "dp"), None),
            P(("comp", "dp"), None),
            P(("comp", "dp")),
        ),
        out_specs=(P(("comp", "dp"), None), P(("comp", "dp"), None), P(("comp", "dp")), P("dp")),
        check_vma=False,
    )
```

```python
import functools

import jax
import jax.numpy as jnp
from jax import lax
from jax.experimental import pallas as pl
from jax.experimental.pallas import tpu as pltpu
from jax.sharding import PartitionSpec as P

circle_log = 1.8378770664093453
MESH = pl.DeviceIdType.MESH
NX = 4
LAG = 1.6
UNIT = 2.8
PAD = 128
IN_STREAMS = ((0, 0.0, 1.0, False), (1, 0.0, 2.0, False))
OUT_STREAMS = ((0, 0.0, 1.0, False), (1, 0.0, 2.0, False))


def columns(stream, width):
    _, lo, hi, _ = stream
    return int(lo * width), width + PAD if hi > 1.0 else int(hi * width)


def weight(stream):
    lo, hi = columns(stream, 1024)
    return (hi - lo) / 1024 * UNIT


def sign(v):
    return (v > 0) - (v < 0)


def canon(d, n):
    d = d % n
    return d if d <= n // 2 else d - n


def hops_on(d, n):
    out = []
    for way in (1, -1):
        if d != 0 and (d > 0) == (way > 0):
            continue
        if abs(d) == n // 2:
            continue
        new = d - way
        if abs(new) < n // 2:
            out.append((way, new, None))
        elif abs(new) == n // 2:
            out.append((way, n // 2, 0 if way > 0 else 1))
    return out


def axes_of(stream):
    return ("x", "z") if stream[3] else ("z", "x")


def gather_sends(stream, df, ds, nf, ns):
    first, second = axes_of(stream)
    out = []
    if ds == 0:
        out += [(first, way, (d, 0, half)) for way, d, half in hops_on(df, nf)]
    out += [(second, way, (df, d, half)) for way, d, half in hops_on(ds, ns)]
    return out


def gather_plan(nx, nz, ny):
    size = {"x": nx, "z": nz}
    free, arrivals, plan = {}, [], []
    t = 0.0
    halves = {}
    left = {(b, dx): nz * sum(s[0] == b for s in IN_STREAMS) for b in (0, 1) for dx in range(nx)}
    rows_left = {canon(y, ny): 4 for y in range(ny)}
    whole, dots, here = [], [], []

    def push(axis, way, work, event):
        start = max(t, free.get((axis, way), 0.0))
        free[(axis, way)] = start + work
        arrivals.append((start + work + LAG, str(event), event))

    def available(k, df, ds):
        stream = IN_STREAMS[k]
        first, second = axes_of(stream)
        for axis, way, slot in gather_sends(stream, df, ds, size[first], size[second]):
            work = weight(stream) * (0.5 if slot[2] is not None else 1.0) * (2 if axis == "z" else 1)
            push(axis, way, work, ("recv", k, slot))
            plan.append(("send", k, (df, ds), axis, way, slot))
        dx = (df if stream[3] else ds) % nx
        left[(stream[0], dx)] -= 1
        if left[(stream[0], dx)] == 0:
            whole.append((stream[0], dx))
            dots.append(("turn", stream[0], dx))
            dots.extend(("dot", stream[0], dx, c) for c in here)

    def rows_on(dy, q):
        for way, new, half in hops_on(dy, ny):
            if half is None or half == q:
                push("y", way, 2 * UNIT, ("rows", "y", new, q))
                plan.append(("rows_send", "y", way, dy, new, q))
        push("c", 1, UNIT / 3, ("rows", "c", dy, q))
        plan.append(("rows_send", "c", 0, dy, dy, q))

    def rows_here(chunk):
        here.append(chunk)
        dots.extend(("dot",) + w + (chunk,) for w in whole)

    def rows_go(q):
        push("z", 1, 2 * UNIT, ("rows", "p", 0, q))
        plan.append(("rows_send", "p", 0, 0, 0, q))

    def rows_after(k, d):
        relays.discard((k, d))
        if not relays and rows_sent == []:
            for q in (0, 1):
                rows_go(q)
                rows_sent.append(q)

    rows_sent = []
    relays = {(k, d) for k in range(len(IN_STREAMS)) for d in ((-1, 1) if nz > 2 else (0,))}
    for k in range(len(IN_STREAMS)):
        available(k, 0, 0)
        rows_after(k, 0)
    plan.append(("split",))
    t += 4.0
    rows_here(None)
    while arrivals or dots:
        arrivals.sort(key=lambda a: a[:2])
        if arrivals and arrivals[0][0] <= t or not dots:
            when, _, event = arrivals.pop(0)
            t = max(t, when)
            plan.append(event)
            if event[0] == "rows":
                if event[1] != "c":
                    rows_on(*event[2:])
                plan.append(("rows_split",) + event[1:])
                t += 0.2
                rows_left[event[2]] -= 1
                if rows_left[event[2]] == 0:
                    rows_here(event[2])
                continue
            _, k, (df, ds, half) = event
            if half is not None:
                halves[(k, df, ds)] = halves.get((k, df, ds), 0) + 1
                if halves[(k, df, ds)] < 2:
                    continue
            available(k, df, ds)
            if ds == 0:
                rows_after(k, df)
        else:
            op = dots.pop(0)
            plan.append(op)
            t += 0.3 if op[0] == "turn" else 1.6 if op[3] is None else 0.45
    return plan


def reduce_inputs(stream, df, ds, nf, ns):
    def along(d, n):
        if d == 0:
            return [(1, None), (-1, None)] if n > 2 else [(1, 0), (1, 1)]
        if abs(d) == n // 2:
            return []
        far = d + sign(d)
        if abs(far) == n // 2:
            return [(n // 2, 0 if d > 0 else 1)]
        return [(far, None)]

    out = [(df, d, half) for d, half in along(ds, ns)]
    if ds == 0:
        out += [(d, 0, half) for d, half in along(df, nf)]
    return out


def reduce_sends(stream, df, ds, nf, ns):
    first, second = axes_of(stream)
    axis, d, n = (second, ds, ns) if ds != 0 else (first, df, nf)
    if d == 0:
        return []
    if abs(d) == n // 2:
        return [(axis, 1, (df, ds, 0)), (axis, -1, (df, ds, 1))]
    return [(axis, sign(d), (df, ds, None))]


def reduce_plan(nx, nz):
    size = {"x": nx, "z": nz}
    free, arrivals, plan = {}, [], []
    t = 0.0
    groups = sorted(range(nx), key=lambda dx: (-abs(canon(dx, nx)), dx))
    done, landed = set(), set()
    waiting = []
    for k, stream in enumerate(OUT_STREAMS):
        first, second = axes_of(stream)
        for f in range(size[first]):
            for s in range(size[second]):
                waiting.append((k, canon(f, size[first]), canon(s, size[second])))

    def is_ready(item):
        k, df, ds = item
        stream = OUT_STREAMS[k]
        first, second = axes_of(stream)
        if (df if stream[3] else ds) % nx not in done:
            return False
        needs = reduce_inputs(stream, df, ds, size[first], size[second])
        return all((k, n) in landed for n in needs)

    while waiting:
        for a in [a for a in arrivals if a[0] <= t]:
            arrivals.remove(a)
            landed.add(a[1:])
        ready = sorted((w for w in waiting if is_ready(w)), key=lambda w: (-abs(w[1]) - abs(w[2]), w))
        if ready:
            item = ready[0]
            waiting.remove(item)
            k, df, ds = item
            stream = OUT_STREAMS[k]
            first, second = axes_of(stream)
            plan.append(("sum", k, (df, ds)))
            t += 0.15
            for axis, way, slot in reduce_sends(stream, df, ds, size[first], size[second]):
                work = weight(stream) * (0.5 if slot[2] is not None else 1.0) * (2 if axis == "z" else 1)
                start = max(t, free.get((axis, way), 0.0))
                free[(axis, way)] = start + work
                arrivals.append((start + work + LAG, k, slot))
        elif groups:
            dx = groups.pop(0)
            plan.append(("moments", dx))
            t += 4.5
            done.add(dx)
        else:
            t = min(a[0] for a in arrivals)
    return plan


class Place:
    def __init__(self, nx, nz, comps):
        self.nx, self.nz, self.ny = nx, nz // 2, comps // 2
        me = lax.axis_index("dp")
        self.x, z = me // nz, me % nz
        self.j, self.parity = z // 2, z % 2
        self.comp = lax.axis_index("comp")
        self.y, self.core = self.comp // 2, self.comp % 2
        self.full_z = nz

    def block(self, dx, dz):
        return ((self.x + dx) % self.nx) * self.nz + (self.j + dz) % self.nz

    def of(self, stream, df, ds):
        return self.block(df, ds) if stream[3] else self.block(ds, df)

    def group(self, dx):
        return (self.x + dx) % self.nx

    def neighbour(self, axis, way):
        x, j = (self.x + way, self.j) if axis == "x" else (self.x, self.j + way)
        return {"dp": (x % self.nx) * self.full_z + 2 * (j % self.nz) + self.parity}

    def partner(self):
        return {"dp": self.x * self.full_z + 2 * self.j + 1 - self.parity}

    def row_target(self, kind, way):
        if kind == "p":
            return self.partner()
        if kind == "y":
            return {"comp": ((self.y + way) % self.ny) * 2 + self.core}
        return {"comp": self.y * 2 + 1 - self.core}

    def slot(self, k, stream, slot):
        df, ds, half = slot
        nf, ns = (self.nx, self.nz) if stream[3] else (self.nz, self.nx)
        return ((k * nf + df % nf) * ns + ds % ns) * 2 + (half or 0)


def part(ref, index, half, cols):
    rows = ref.shape[1]
    at = pl.ds(0, rows) if half is None else pl.ds(half * (rows // 2), rows // 2)
    return ref.at[index, at, pl.ds(cols[0], cols[1] - cols[0])]


def split(x):
    high = x.astype(jnp.bfloat16)
    return high, (x - high.astype(jnp.float32)).astype(jnp.bfloat16)


def dot_nt(a, b):
    return lax.dot_general(a, b, (((1,), (1,)), ((), ())), preferred_element_type=jnp.float32)


def dot_nn(a, b):
    return jnp.dot(a, b, preferred_element_type=jnp.float32)


def kernel(
    nx, nz, comps, x_hbm, means_ref, var_ref, logw_ref, new_means_ref, new_var_ref, weight_ref, loglik_ref,
    scaled, prec, other, x_ref, xh, xl, qh, ql, pt, scores, stat, norm, rh, rl,
    sum_a, sum_b, land_a, land_b,
    in_send, in_recv, out_send, out_recv, row_send, row_recv, stat_send, stat_recv, load_sem,
):
    place = Place(nx, nz, comps)
    nz, ny = place.nz, place.ny
    rows, width = x_ref.shape
    size = means_ref.shape[0]
    load = pltpu.make_async_copy(x_hbm, x_ref, load_sem)
    load.start()
    group = nz * size
    own = place.block(0, 0)
    parity, comp = place.parity, place.comp
    own_rows = pl.multiple_of(parity * rows, rows)
    other_rows = pl.multiple_of((1 - parity) * rows, rows)
    sub = rows // comps // 2
    variances = var_ref[...]
    means = means_ref[...]
    p = 1.0 / variances
    sc = means * p
    diagonal = lax.broadcasted_iota(jnp.int32, (size, size), 0) == lax.broadcasted_iota(jnp.int32, (size, size), 1)
    offset = (
        jnp.sum(jnp.where(diagonal, logw_ref[...], 0.0), axis=1, keepdims=True)
        - 0.5 * jnp.sum(jnp.log(variances), axis=1, keepdims=True)
        - 0.5 * jnp.sum(means * sc, axis=1, keepdims=True)
    )
    scaled[own] = sc
    prec[own, :, 0:width] = -0.5 * (p - 1.0)
    prec[own, :, width : width + PAD] = jnp.broadcast_to(offset, (size, PAD))

    barrier = pltpu.get_barrier_semaphore()
    friends = [place.neighbour(axis, way) for axis in ("x", "z") for way in (1, -1)]
    friends += [{"comp": (comp + k) % comps} for k in range(1, comps)]
    friends += [dict(place.partner(), comp=(comp + k) % comps) for k in range(comps)]
    for friend in friends:
        pl.semaphore_signal(barrier, inc=1, device_id=friend, device_id_type=MESH)
    pl.semaphore_wait(barrier, len(friends))
    load.wait()

    started = []

    def begin(c):
        c.start()
        started.append(c)

    def remote(src, dst, send, recv, target):
        return pltpu.make_async_remote_copy(
            src_ref=src, dst_ref=dst, send_sem=send, recv_sem=recv, device_id=target, device_id_type=MESH
        )

    bufs = (scaled, prec)

    def param_copy(k, offs, axis, way, slot):
        stream = IN_STREAMS[k]
        n = place.slot(k, stream, slot)
        ref = part(bufs[stream[0]], place.of(stream, *offs), slot[2], columns(stream, width))
        return remote(ref, ref, in_send.at[n], in_recv.at[n], place.neighbour(axis, way))

    def slice_of(kind, dy, q):
        core = 1 - place.core if kind == "c" else place.core
        return (((place.y + dy) % ny) * 2 + core) * 2 + q

    def row_sem(kind, new, q):
        return ((("p", "y", "c").index(kind)) * ny + new % ny) * 2 + q

    def row_copy(kind, way, dy, new, q):
        index = slice_of("p", dy, q)
        n = row_sem(kind, new, q)
        if kind == "p":
            src = x_ref.at[pl.ds(pl.multiple_of(index * sub, sub), sub), :]
        else:
            src = other.at[index]
        return remote(src, other.at[index], row_send.at[n], row_recv.at[n], place.row_target(kind, way))

    def split_into(base, x):
        at = pl.ds(base, x.shape[0])
        xh[at, :], xl[at, :] = split(x)
        qh[at, :], ql[at, :] = split(x * x)

    ones = jnp.ones((8, width), jnp.bfloat16)
    begun = set()
    formed = set()
    for op in gather_plan(nx, nz, ny):
        if op[0] == "send":
            begin(param_copy(*op[1:]))
        elif op[0] == "recv":
            _, k, slot = op
            param_copy(k, slot[:2], "x", 1, slot).wait_recv()
        elif op[0] == "rows_send":
            begin(row_copy(*op[1:]))
        elif op[0] == "rows":
            _, kind, dy, q = op
            ref = other.at[slice_of(kind, dy, q)]
            n = row_sem(kind, dy, q)
            remote(ref, ref, row_send.at[n], row_recv.at[n], place.partner()).wait_recv()
        elif op[0] == "rows_split":
            _, kind, dy, q = op
            index = slice_of(kind, dy, q)
            split_into(pl.multiple_of(other_rows + index * sub, sub), other[index])
        elif op[0] == "split":
            few = min(64, rows)

            @pl.loop(0, rows // few)
            def _(i):
                at = pl.multiple_of(i * few, few)
                split_into(pl.multiple_of(own_rows + at, few), x_ref[pl.ds(at, few), :])

            few = min(256, rows)

            @pl.loop(0, rows // few)
            def _(i):
                n = pl.ds(pl.multiple_of(own_rows + i * few, few), few)
                here = pl.ds(pl.multiple_of(i * few, few), few)
                square = dot_nt(ones, qh[n, :]) + dot_nt(ones, ql[n, :])
                loglik_ref[:, here] = 0.5 * square[0:1, :] + 0.5 * width * circle_log
        elif op[0] == "turn":
            _, b, dx = op
            blocks = pl.ds(pl.multiple_of(place.group(dx) * nz, nz), nz)
            turned = bufs[b][blocks, :, 0:width].reshape(group, width).T
            pt[b * nx + dx, :, 0:group], pt[b * nx + dx, :, group : 2 * group] = split(turned)
        else:
            _, b, dx, h = op
            g = place.group(dx)
            blocks = pl.ds(pl.multiple_of(g * nz, nz), nz)
            at = pl.ds(pl.multiple_of(g * group, group), group)
            params = pt.at[b * nx + dx]
            high, low = (xh, xl) if b == 0 else (qh, ql)
            last = (dx, h) in formed
            formed.add((dx, h))
            opening = last and h not in begun
            if last:
                begun.add(h)
            many = 4 * sub
            base = own_rows if h is None else other_rows + ((place.y + h) % ny) * many
            count = rows if h is None else many
            tile = min(256, count)

            @pl.loop(0, count // tile)
            def _(i):
                n = pl.ds(pl.multiple_of(base + i * tile, tile), tile)
                both = dot_nn(high[n, :], params[...])
                s = both[:, 0:group] + both[:, group : 2 * group] + dot_nn(low[n, :], params[:, 0:group])
                s = s.T
                if not last:
                    scores[at, n] = s
                    return
                off = prec[blocks, :, width : width + PAD].reshape(group, PAD)[:, 0:1]
                s = s + scores[at, n] + off
                scores[at, n] = s
                peak = jnp.max(s, axis=0, keepdims=True)
                if opening:
                    norm[0:1, n] = peak
                    norm[1:2, n] = jnp.sum(jnp.exp(s - peak), axis=0, keepdims=True)
                else:
                    before = norm[0:1, n]
                    now = jnp.maximum(before, peak)
                    norm[1:2, n] = norm[1:2, n] * jnp.exp(before - now) + jnp.sum(
                        jnp.exp(s - now), axis=0, keepdims=True
                    )
                    norm[0:1, n] = now

    mine = parity * comps + comp
    stat[mine] = norm[0:2, :]
    peers = [(0, k) for k in range(1, comps)] + [(1, k) for k in range(comps)]
    for other_z, k in peers:
        target = {"comp": (comp + k) % comps}
        if other_z:
            target.update(place.partner())
        n = other_z * comps + k
        begin(remote(stat.at[mine], stat.at[mine], stat_send.at[n], stat_recv.at[n], target))

    for other_z, k in peers:
        source = ((1 - parity) if other_z else parity) * comps + (comp - k + comps) % comps
        n = other_z * comps + k
        ref = stat.at[source]
        remote(ref, ref, stat_send.at[n], stat_recv.at[n], place.partner()).wait_recv()
    peak = stat[0, 0:1, :]
    for c in range(1, 2 * comps):
        peak = jnp.maximum(peak, stat[c, 0:1, :])
    total = jnp.zeros_like(peak)
    for c in range(2 * comps):
        total = total + stat[c, 1:2, :] * jnp.exp(stat[c, 0:1, :] - peak)
    norm[0:1, :] = peak + jnp.log(total)
    loglik_ref[...] = norm[0:1, pl.ds(own_rows, rows)] - loglik_ref[...]

    sums, lands = (sum_a, sum_b), (land_a, land_b)

    def sum_copy(k, axis, way, slot):
        stream = OUT_STREAMS[k]
        df, ds, half = slot
        b, cols = stream[0], columns(stream, width)
        n = place.slot(k, stream, slot)
        return remote(
            part(sums[b], place.of(stream, df, ds), half, cols),
            part(lands[b], landing(k, slot), half, cols),
            out_send.at[n],
            out_recv.at[n],
            place.neighbour(axis, way),
        )

    def landing(k, slot):
        return place.slot(0, OUT_STREAMS[k], slot) // 2

    for op in reduce_plan(nx, nz):
        if op[0] == "moments":
            g = place.group(op[1])
            base = g * nz

            @pl.loop(0, nz)
            def _(i):
                at = pl.ds(pl.multiple_of(g * group + i * size, size), size)
                here = pl.ds(pl.multiple_of(i * size, size), size)
                r = jnp.exp(scores[at, :] - norm[0:1, :])
                rh[here, :], rl[here, :] = split(r)
                counts = jnp.sum(r, axis=1, keepdims=True)
                sum_b[base + i, :, width : width + PAD] = jnp.broadcast_to(counts, (size, PAD))

            blocks = pl.ds(pl.multiple_of(base, nz), nz)
            cols = min(256, width)

            @pl.loop(0, width // cols)
            def _(i):
                d = pl.ds(pl.multiple_of(i * cols, cols), cols)
                a = dot_nn(rh[...], xh[:, d]) + dot_nn(rh[...], xl[:, d]) + dot_nn(rl[...], xh[:, d])
                sum_a[blocks, :, d] = a.reshape(nz, size, cols)
                b = dot_nn(rh[...], qh[:, d]) + dot_nn(rh[...], ql[:, d]) + dot_nn(rl[...], qh[:, d])
                sum_b[blocks, :, d] = b.reshape(nz, size, cols)
            continue
        _, k, (df, ds) = op
        stream = OUT_STREAMS[k]
        nf, ns = (nx, nz) if stream[3] else (nz, nx)
        index = place.of(stream, df, ds)
        whole, cut = [], []
        for slot in reduce_inputs(stream, df, ds, nf, ns):
            sum_copy(k, "x", 1, slot).wait_recv()
            (whole if slot[2] is None else cut).append(slot)
        lo, hi = columns(stream, width)
        out, land = sums[stream[0]], lands[stream[0]]
        if whole:
            v = out[index, :, lo:hi]
            for slot in whole:
                v = v + land[landing(k, slot), :, lo:hi]
            out[index, :, lo:hi] = v
        for slot in cut:
            at = pl.ds(slot[2] * (size // 2), size // 2)
            out[index, at, lo:hi] = out[index, at, lo:hi] + land[landing(k, slot), at, lo:hi]
        for axis, way, slot in reduce_sends(stream, df, ds, nf, ns):
            begin(sum_copy(k, axis, way, slot))
    counts = sum_b[own, :, width : width + 1]
    denom = counts + 1.0
    means = means_ref[...]
    new_means = (sum_a[own] + means) / denom
    new_means_ref[...] = new_means
    new_var_ref[...] = (sum_b[own, :, 0:width] + var_ref[...] + means * means) / denom - new_means * new_means
    weight_ref[...] = jnp.sum(jnp.where(diagonal, counts, 0.0), axis=0, keepdims=True) / (rows * nx * place.full_z)
    for c in started:
        c.wait_send()


def per_device(nx, nz, comps, x, means, variances, log_weights):
    rows, width = x.shape
    size = means.shape[0]
    count = nx * nz // 2
    group = nz // 2 * size
    vmem = pl.BlockSpec(memory_space=pltpu.VMEM)
    f32, bf16 = jnp.float32, jnp.bfloat16
    dma = pltpu.SemaphoreType.DMA
    new_means, new_variances, new_weights, loglik = pl.pallas_call(
        functools.partial(kernel, nx, nz, comps),
        out_shape=(
            jax.ShapeDtypeStruct((size, width), f32),
            jax.ShapeDtypeStruct((size, width), f32),
            jax.ShapeDtypeStruct((1, size), f32),
            jax.ShapeDtypeStruct((1, rows), f32),
        ),
        in_specs=[pl.BlockSpec(memory_space=pl.ANY)] + [vmem] * 3,
        out_specs=(vmem,) * 4,
        scratch_shapes=[
            pltpu.VMEM((count, size, width), f32),
            pltpu.VMEM((count, size, width + PAD), f32),
            pltpu.VMEM((2 * comps, rows // comps // 2, width), f32),
            pltpu.VMEM((rows, width), f32),
            *[pltpu.VMEM((2 * rows, width), bf16)] * 4,
            pltpu.VMEM((2 * nx, width, 2 * group), bf16),
            pltpu.VMEM((count * size, 2 * rows), f32),
            pltpu.VMEM((2 * comps, 2, 2 * rows), f32),
            pltpu.VMEM((8, 2 * rows), f32),
            *[pltpu.VMEM((group, 2 * rows), bf16)] * 2,
            *[pltpu.VMEM((count, size, width), f32), pltpu.VMEM((count, size, width + PAD), f32)] * 2,
            *[dma((2 * count * len(IN_STREAMS),))] * 2,
            *[dma((2 * count * len(OUT_STREAMS),))] * 2,
            *[dma((3 * comps,))] * 2,
            *[dma((2 * comps,))] * 2,
            dma,
        ],
        compiler_params=pltpu.CompilerParams(
            collective_id=0, has_side_effects=True, vmem_limit_bytes=60 << 20
        ),
        name="mixture",
    )(x, means, variances, log_weights[None, :])
    return (new_means, new_variances, new_weights.reshape(size), loglik.reshape(rows))


def solution(mesh):
    count, comps = mesh.shape["dp"], mesh.shape["comp"]
    return jax.shard_map(
        functools.partial(per_device, NX, count // NX, comps),
        mesh=mesh,
        in_specs=(
            P("dp", None),
            P(("comp", "dp"), None),
            P(("comp", "dp"), None),
            P(("comp", "dp")),
        ),
        out_specs=(P(("comp", "dp"), None), P(("comp", "dp"), None), P(("comp", "dp")), P("dp")),
        check_vma=False,
    )
```
